256 devices in a mesh: gx: 8 (over y, core), gy: 8 (over z), gz: 4 (over x).
Axes of the slice: x: 4, y: 4, z: 8, core: 2. Of those that a mesh axis runs over, the one named last changes fastest.
Arguments:
- right_side: float32 [128, 128, 512], P('gx', 'gy', 'gz'), may hold values from -5 to 5, as said below
- conductivity: float32 [128, 128, 512], P('gx', 'gy', 'gz'), may hold values from 0.1 to 10
Outputs:
- solution: float32 [128, 128, 512], P('gx', 'gy', 'gz')
The draws below stay inside these ranges and needn't reach their ends.
Inputs may be any that keep to these rules, and one draw needn't show every extreme that they name: `right_side`: a source field of order one.
All inputs are finite; a program needn't handle non-finite values.
Results may differ from the reference program's by a relative error of at most 0.0001.
Values sent between devices are 32-bit elements; how exact they have to be, the bound alone decides.
No kernel may reach another device: no remote copies, remote signals or barrier semaphores. Data moves between devices by JAX's collectives and lax.ppermute only.
A program may use at most 64 MiB of HBM per device.

```python
import math
import jax
import jax.numpy as jnp

COARSE = 8
SWEEPS = 4
CSWEEPS = 8
CYCLES = 2
NX = 128
NY = 128
NZ = 512


def spread_ends(values):
    highest = jnp.maximum(jnp.max(values), 0.5)
    lowest = jnp.maximum(-jnp.min(values), 0.5)
    scaled = jnp.where(values > 0, values * (5.0 / highest), values * (5.0 / lowest))
    return jnp.clip(scaled, -5.0, 5.0)


def draw_right_side(key, part):
    values = jax.random.normal(key, (NX, NY, NZ), jnp.float32)
    return spread_ends(values)


def steps_of(own_key, shape, cuts, smallest, high):
    factor_of, own = 1.0, jax.random.fold_in(own_key, 6)
    for dim, shards_of in cuts:
        heights = jnp.exp(jax.random.uniform(jax.random.fold_in(own, dim), (shards_of,), jnp.float32, smallest / len(cuts), high / len(cuts)))
        factor_of = factor_of * jnp.repeat(heights, shape[dim] // shards_of).reshape([-1 if axis == dim else 1 for axis in range(len(shape))])
    return factor_of


def setup_inputs(seed: int = 0) -> dict:
    streams_of = jax.random.split(jax.random.key(seed), 3)
    return {
        "right_side": draw_right_side(jax.random.fold_in(streams_of[2], 71), 0),
        "conductivity": jnp.clip(jnp.exp(math.log(10.0) - 4.6051702 * jax.random.uniform(streams_of[1], (NX, NY, NZ), jnp.float32) ** steps_of(streams_of[1], (NX, NY, NZ), ((0, 8), (1, 8), (2, 4)), -0.2, 0.2)), 0.1, 10.0),
    }


omega_weight = 0.8


def stencil_coefs(conduct):
    padded = jnp.pad(conduct, 1)
    face_west = 0.5 * (conduct + padded[:-2, 1:-1, 1:-1])
    face_east = 0.5 * (conduct + padded[2:, 1:-1, 1:-1])
    face_south = 0.5 * (conduct + padded[1:-1, :-2, 1:-1])
    face_north = 0.5 * (conduct + padded[1:-1, 2:, 1:-1])
    face_below = 0.5 * (conduct + padded[1:-1, 1:-1, :-2])
    face_above = 0.5 * (conduct + padded[1:-1, 1:-1, 2:])
    diagonal = ((face_west + face_east) + (face_south + face_north)) + (face_below + face_above)
    return (face_west, face_east, face_south, face_north, face_below, face_above, diagonal)


def apply_operator(values, stencil):
    face_west, face_east, face_south, face_north, face_below, face_above, diagonal = stencil
    padded = jnp.pad(values, 1)
    nearby = face_west * padded[:-2, 1:-1, 1:-1] + face_east * padded[2:, 1:-1, 1:-1]
    nearby = nearby + face_south * padded[1:-1, :-2, 1:-1] + face_north * padded[1:-1, 2:, 1:-1]
    nearby = nearby + face_below * padded[1:-1, 1:-1, :-2] + face_above * padded[1:-1, 1:-1, 2:]
    return diagonal * values - nearby


def jacobi(values, source, stencil, inside, repeats):
    safe_diag = jnp.where(inside, stencil[6], 1.0)
    for sweep_step in range(repeats):
        update = values + omega_weight * (source - apply_operator(values, stencil)) / safe_diag
        values = jnp.where(inside, update, 0.0)
    return values


def restrict(values, factor):
    extent = values.shape
    blocks = values.reshape(extent[0] // factor, factor, extent[1] // factor, factor, extent[2] // factor, factor)
    return blocks.sum(axis=(1, 3, 5))


def prolong(values, factor):
    extent = values.shape
    spread = jnp.broadcast_to(values[:, None, :, None, :, None], (extent[0], factor, extent[1], factor, extent[2], factor))
    return spread.reshape(extent[0] * factor, extent[1] * factor, extent[2] * factor)


def reference(right_side, conductivity):
    stencil = stencil_coefs(conductivity)
    coarse_stencil = stencil_coefs(restrict(conductivity, COARSE) / (COARSE * COARSE))
    solution = jnp.zeros_like(right_side)
    for cycle_step in range(CYCLES):
        solution = jacobi(solution, right_side, stencil, True, SWEEPS)
        residual = right_side - apply_operator(solution, stencil)
        coarse_rhs = restrict(residual, COARSE)
        correction = jacobi(jnp.zeros_like(coarse_rhs), coarse_rhs, coarse_stencil, True, CSWEEPS)
        solution = solution + prolong(correction, COARSE)
        solution = jacobi(solution, right_side, stencil, True, SWEEPS)
    return solution
```

```python
import functools

import jax
import jax.numpy as jnp
from jax import lax
from jax.experimental import pallas as pl
from jax.experimental.pallas import tpu as pltpu
from jax.sharding import PartitionSpec as P

SWEEPS = 4
CSWEEPS = 8
OMEGA = 0.8
KEEP = 0.2
AXES = ("gx", "gy", "gz")
NGX, NGY, NGZ = 8, 8, 4
BX, BY, BZ = 16, 16, 128
HALO = 8
PLANES = BZ + 2 * HALO
CHUNK = 8
CHUNKS = PLANES // CHUNK
STEP = CHUNK * 8
ROWS = PLANES * 8
PADDED = ROWS + 2 * STEP
DEVICES = NGX * NGY * NGZ
EDGE = 40
F32 = jnp.float32
EXACT = lax.Precision.HIGHEST
VMEM_LIMIT = 24 * 1024 * 1024


def call(kernel, outs, scratch, *args):
    return pl.pallas_call(
        kernel,
        out_shape=[jax.ShapeDtypeStruct(shape, F32) for shape in outs],
        in_specs=[pl.BlockSpec(memory_space=pltpu.VMEM)] * len(args),
        out_specs=[pl.BlockSpec(memory_space=pltpu.VMEM)] * len(outs),
        scratch_shapes=[pltpu.VMEM(shape, F32) for shape in scratch],
        compiler_params=pltpu.CompilerParams(vmem_limit_bytes=VMEM_LIMIT),
    )(*args)


def iota(shape, dim):
    return lax.broadcasted_iota(jnp.int32, shape, dim)


def east(v):
    turned = pltpu.roll(v, 96, 2)
    return jnp.where(iota(v.shape, 2) < 96, turned, pltpu.roll(turned, 7, 1))


def west(v):
    turned = pltpu.roll(v, 32, 2)
    return jnp.where(iota(v.shape, 2) >= 32, turned, pltpu.roll(turned, 1, 1))


def north(v):
    return pltpu.roll(v, 127, 2)


def south(v):
    return pltpu.roll(v, 1, 2)


def planes(ref, row, size=STEP):
    return ref[pl.ds(pl.multiple_of(row, 8), size), :].reshape(size // 8, 8, 128)


def put(ref, row, value):
    ref[pl.ds(pl.multiple_of(row, 8), value.shape[0] * 8), :] = value.reshape(-1, 128)


def turn_kernel(count, own_lo, own_hi, y_lo, y_hi, x_lo, x_hi, out, z_lo, z_hi):
    for a in range(count):
        for sub in range(8):
            if sub < 2:
                block = x_lo[a, 4 * sub : 4 * sub + 4].reshape(128, 128)
            elif sub >= 6:
                block = x_hi[a, 4 * sub - 24 : 4 * sub - 20].reshape(128, 128)
            else:
                pieces = []
                for x in range(4 * sub - 8, 4 * sub - 4):
                    pieces += [y_lo[a, x], own_lo[a, x], own_hi[a, x], y_hi[a, x]]
                block = jnp.concatenate(pieces, axis=0)
            turned = block.T
            out[a, pl.ds(sub, BZ, stride=8), :] = turned
            z_lo[a, pl.ds(sub, HALO, stride=8), :] = turned[:HALO]
            z_hi[a, pl.ds(sub, HALO, stride=8), :] = turned[BZ - HALO :]


def turn(own_lo, own_hi, y_lo, y_hi, x_lo, x_hi):
    count = own_lo.shape[0]
    return call(
        functools.partial(turn_kernel, count),
        [(count, BZ * 8, 128), (count, STEP, 128), (count, STEP, 128)],
        [],
        own_lo, own_hi, y_lo, y_hi, x_lo, x_hi,
    )


def sweep(src, dst, coefs, source):
    def body(k, _):
        row = pl.multiple_of(k * STEP, STEP)
        v = planes(src, row + STEP)
        total = KEEP * v + planes(source, row)
        total = total + neighbours(src, v, coefs, row)
        put(dst, row + STEP, total)
        return 0

    lax.fori_loop(0, CHUNKS, body, 0)


def neighbours(src, v, coefs, row):
    hxm, hxp, hym, hyp, hzm, hzp = (planes(ref, row) for ref in coefs)
    total = hzm * planes(src, row + STEP - 8) + hzp * planes(src, row + STEP + 8)
    total = total + (hxm * west(v) + hxp * east(v))
    return total + (hym * south(v) + hyp * north(v))


def clear_ends(*refs):
    for ref in refs:
        ref[pl.ds(0, STEP), :] = jnp.zeros((STEP, 128), F32)
        ref[pl.ds(ROWS + STEP, STEP), :] = jnp.zeros((STEP, 128), F32)


def coarse_pieces(layers):
    lane = iota((16, 128), 1) % 32
    pieces = []
    for i in range(2):
        first = layers[pl.ds(2 + 2 * i, 16, stride=8), :]
        row = first + layers[pl.ds(3 + 2 * i, 16, stride=8), :]
        for j in range(2):
            pieces.append(jnp.where(lane // 8 == 1 + j, row, 0.0))
    return pieces


def send_rows(send, left, right):
    table = jnp.concatenate(left + right, axis=0)
    line = lax.dot_general(
        jnp.ones((8, 128), F32), table, (((1,), (1,)), ((), ())),
        precision=EXACT, preferred_element_type=F32,
    )
    send[...] = jnp.concatenate([line] * (DEVICES // 8), axis=0)


def residual_layers(src, coefs, source, weight, layers):
    def body(k, _):
        row = pl.multiple_of(k * STEP + STEP, STEP)
        v = planes(src, row + STEP)
        rest = planes(source, row) + neighbours(src, v, coefs, row) - OMEGA * v
        rest = rest * planes(weight, row)
        layers[pl.ds(pl.multiple_of(k * 8, 8), 8), :] = rest.sum(axis=0)
        return 0

    lax.fori_loop(0, CHUNKS - 2, body, 0)


def first_kernel(
    own, z_lo, z_hi, hxm, hxp, hym, hyp, hzm, hzp, source, weight, u_out, send, cond, buf, layers, clayers
):
    gx, gy, gz = (lax.axis_index(name) for name in AXES)
    shape = (8, 8, 128)
    gxc = gx * BX - HALO + 4 * iota(shape, 1) + iota(shape, 2) // 32
    gyc = gy * BY - HALO + iota(shape, 2) % 32
    inside = (gxc >= 0) & (gxc < NGX * BX) & (gyc >= 0) & (gyc < NGY * BY)
    clear_ends(cond, buf, u_out)

    def load(k, lo, hi, mid):
        return lo, hi, mid

    put(cond, STEP, jnp.where(inside & (gz > 0), planes(z_lo.at[1], 0), 0.0))
    put(cond, ROWS, jnp.where(inside & (gz < NGZ - 1), planes(z_hi.at[1], 0), 0.0))
    put(source, 0, planes(z_lo.at[0], 0))
    put(source, ROWS - STEP, planes(z_hi.at[0], 0))

    def fill(k, _):
        row = pl.multiple_of(k * STEP, STEP)
        c = planes(own.at[1], row)
        put(cond, row + 2 * STEP, jnp.where(inside, c, 0.0))
        clayers[pl.ds(pl.multiple_of(k * 8, 8), 8), :] = c.sum(axis=0)
        put(source, row + STEP, planes(own.at[0], row))
        return 0

    lax.fori_loop(0, CHUNKS - 2, fill, 0)

    def coefs_of(k, _):
        row = pl.multiple_of(k * STEP, STEP)
        c = planes(cond, row + STEP)
        fxm, fxp = 0.5 * (c + west(c)), 0.5 * (c + east(c))
        fym, fyp = 0.5 * (c + south(c)), 0.5 * (c + north(c))
        fzm = 0.5 * (c + planes(cond, row + STEP - 8))
        fzp = 0.5 * (c + planes(cond, row + STEP + 8))
        diag = ((fxm + fxp) + (fym + fyp)) + (fzm + fzp)
        gzc = gz * BZ - HALO + k * CHUNK + iota(shape, 0)
        here = inside & (gzc >= 0) & (gzc < NGZ * BZ)
        w = jnp.where(here, OMEGA / jnp.where(here, diag, 1.0), 0.0)
        put(hxm, row, jnp.where(gxc > 0, w * fxm, 0.0))
        put(hxp, row, jnp.where(gxc < NGX * BX - 1, w * fxp, 0.0))
        put(hym, row, jnp.where(gyc > 0, w * fym, 0.0))
        put(hyp, row, jnp.where(gyc < NGY * BY - 1, w * fyp, 0.0))
        put(hzm, row, jnp.where(gzc > 0, w * fzm, 0.0))
        put(hzp, row, jnp.where(gzc < NGZ * BZ - 1, w * fzp, 0.0))
        g = w * planes(source, row)
        put(source, row, g)
        put(weight, row, diag * (1.0 / OMEGA))
        put(buf, row + STEP, g)
        return 0

    lax.fori_loop(0, CHUNKS, coefs_of, 0)
    coefs = (hxm, hxp, hym, hyp, hzm, hzp)
    sweep(buf, u_out, coefs, source)
    sweep(u_out, buf, coefs, source)
    sweep(buf, u_out, coefs, source)
    residual_layers(u_out, coefs, source, weight, layers)
    scaled = [piece * (1.0 / 64.0) for piece in coarse_pieces(clayers)]
    send_rows(send, coarse_pieces(layers), scaled)


def second_kernel(
    own, z_lo, z_hi, hxm, hxp, hym, hyp, hzm, hzp, source, weight, u_out, send, buf, layers
):
    clear_ends(buf, u_out)
    put(u_out, STEP, planes(z_lo.at[0], 0))
    put(u_out, ROWS, planes(z_hi.at[0], 0))

    def fill(k, _):
        row = pl.multiple_of(k * STEP, STEP)
        put(u_out, row + 2 * STEP, planes(own.at[0], row))
        return 0

    lax.fori_loop(0, CHUNKS - 2, fill, 0)
    coefs = (hxm, hxp, hym, hyp, hzm, hzp)
    sweep(u_out, buf, coefs, source)
    sweep(buf, u_out, coefs, source)
    sweep(u_out, buf, coefs, source)
    sweep(buf, u_out, coefs, source)
    residual_layers(u_out, coefs, source, weight, layers)
    pieces = coarse_pieces(layers)
    send_rows(send, pieces, pieces)


def turn_rows(v, by):
    return pltpu.roll(v, by % DEVICES, 0)


def turn_lanes(v, by):
    return pltpu.roll(v, by % 128, 1)


def coarse_neighbours(e):
    lane = iota((DEVICES, 128), 1)
    low_i, low_j, k = (lane // 32) % 2 == 0, (lane // 16) % 2 == 0, lane % 16
    half = turn_lanes(e, 32)
    xp = jnp.where(low_i, half, turn_rows(half, -32))
    xm = jnp.where(low_i, turn_rows(half, 32), half)
    ahead, behind = turn_lanes(e, -16), turn_lanes(e, 16)
    yp = jnp.where(low_j, ahead, turn_rows(behind, -4))
    ym = jnp.where(low_j, turn_rows(ahead, 4), behind)
    zp = jnp.where(k < 15, turn_lanes(e, -1), turn_rows(turn_lanes(e, 15), -1))
    zm = jnp.where(k > 0, turn_lanes(e, 1), turn_rows(turn_lanes(e, -15), 1))
    return xm, xp, ym, yp, zm, zp


def coarse_open():
    row, lane = iota((DEVICES, 128), 0), iota((DEVICES, 128), 1)
    x = 2 * (row // 32) + (lane // 32) % 2
    y = 2 * ((row // 4) % 8) + (lane // 16) % 2
    z = 16 * (row % 4) + lane % 16
    return x > 0, x < 2 * NGX - 1, y > 0, y < 2 * NGY - 1, z > 0, z < 16 * NGZ - 1


def correct_kernel(
    first, rhs, u, hxm, hxp, hym, hyp, hzm, hzp, source, out_lo, out_hi, buf, other, cc, cg, ext, corr
):
    gx, gy, gz = (lax.axis_index(name) for name in AXES)
    lane = iota((DEVICES, 128), 1)
    cond = first[...]
    cond = jnp.where(lane >= 64, cond, turn_lanes(cond, 64))
    load = rhs[...]
    load = jnp.where(lane < 64, load, turn_lanes(load, 64))
    faces = [
        0.5 * (cond + jnp.where(open_side, near, 0.0))
        for open_side, near in zip(coarse_open(), coarse_neighbours(cond))
    ]
    diag = ((faces[0] + faces[1]) + (faces[2] + faces[3])) + (faces[4] + faces[5])
    w = OMEGA / diag
    for n, (face, open_side) in enumerate(zip(faces, coarse_open())):
        cc[n] = jnp.where(open_side, w * face, 0.0)
    cg[...] = w * load
    zeros = jnp.zeros((EDGE, 128), F32)
    ext[pl.ds(0, EDGE), :] = zeros
    ext[pl.ds(EDGE + DEVICES, EDGE), :] = zeros
    ext[pl.ds(EDGE, DEVICES), :] = cg[...]

    def coarse_sweep(n, _):
        e = ext[pl.ds(EDGE, DEVICES), :]
        total = KEEP * e + cg[...]
        for m, near in enumerate(coarse_neighbours(e)):
            total = total + cc[m] * near
        ext[pl.ds(EDGE, DEVICES), :] = total
        return 0

    lax.fori_loop(0, CSWEEPS - 1, coarse_sweep, 0)

    me = (gx * NGY + gy) * NGZ + gz + EDGE
    span = iota((1, 128), 1)
    lines = []
    for a, i in ((-1, 1), (0, 0), (0, 1), (1, 0)):
        for b, j in ((-1, 1), (0, 0), (0, 1), (1, 0)):
            start = i * 32 + j * 16
            at = me + a * 32 + b * 4
            below = turn_lanes(ext[pl.ds(at - 1, 1), :], -start - 15)
            middle = turn_lanes(ext[pl.ds(at, 1), :], 1 - start)
            above = turn_lanes(ext[pl.ds(at + 1, 1), :], 17 - start)
            lines.append(jnp.where(span == 0, below, jnp.where(span < 17, middle, above)))
    lines.append(jnp.zeros((112, 128), F32))
    grid = jnp.concatenate(lines, axis=0).T[:24]
    for n in range(4):
        pick = (iota((128, 128), 0) == 4 * n + (iota((128, 128), 1) % 32) // 8).astype(F32)
        spread = jnp.dot(grid, pick, precision=EXACT, preferred_element_type=F32)
        corr[pl.ds(2 * n, 24, stride=8), :] = spread
        corr[pl.ds(2 * n + 1, 24, stride=8), :] = spread

    clear_ends(buf, other)

    def add(k, _):
        row = pl.multiple_of(k * STEP, STEP)
        put(buf, row + STEP, planes(u, row + STEP) + planes(corr, k * 8, 8))
        return 0

    lax.fori_loop(0, CHUNKS, add, 0)
    coefs = (hxm, hxp, hym, hyp, hzm, hzp)
    sweep(buf, other, coefs, source)
    sweep(other, buf, coefs, source)
    sweep(buf, other, coefs, source)
    sweep(other, buf, coefs, source)
    for sub in range(2, 6):
        block = buf[pl.ds(2 * STEP + sub, BZ, stride=8), :].T
        for g in range(4):
            x = 4 * sub - 8 + g
            out_lo[0, x] = block[32 * g + 8 : 32 * g + 16]
            out_hi[0, x] = block[32 * g + 16 : 32 * g + 24]


def ring(value, axis, size, by):
    return lax.ppermute(value, axis, [(n, (n + by) % size) for n in range(size)])


def from_both(low, high, axis, size):
    return ring(high, axis, size, 1), ring(low, axis, size, -1)


def spread_planes(own_lo, own_hi):
    y_lo, y_hi = from_both(own_lo, own_hi, "gy", NGY)
    lows = [part[:, :8] for part in (y_lo, own_lo, own_hi, y_hi)]
    highs = [part[:, 8:] for part in (y_lo, own_lo, own_hi, y_hi)]
    x_lo, x_hi = from_both(
        jnp.concatenate(lows, axis=2), jnp.concatenate(highs, axis=2), "gx", NGX
    )
    own, z_lo, z_hi = turn(own_lo, own_hi, y_lo, y_hi, x_lo, x_hi)
    return (own, *from_both(z_lo, z_hi, "gz", NGZ))


def everywhere(send):
    return lax.all_to_all(send, AXES, 0, 0, tiled=True)


def correct(first, rhs, u, coefs, source):
    return call(
        correct_kernel,
        [(1, BX, 8, 128)] * 2,
        [
            (PADDED, 128), (PADDED, 128), (6, DEVICES, 128), (DEVICES, 128),
            (DEVICES + 2 * EDGE, 128), (24 * 8, 128),
        ],
        first, rhs, u, *coefs, source,
    )


def body(right_side, conductivity):
    both = jnp.stack([right_side, conductivity])
    fields = spread_planes(both[:, :, :8], both[:, :, 8:])
    *coefs, source, weight, u, send = call(
        first_kernel,
        [(ROWS, 128)] * 8 + [(PADDED, 128), (DEVICES, 128)],
        [(PADDED, 128), (PADDED, 128), (128, 128), (128, 128)],
        *fields,
    )
    first = everywhere(send)
    halves = correct(first, first, u, coefs, source)
    fields = spread_planes(*halves)
    u, send = call(
        second_kernel,
        [(PADDED, 128), (DEVICES, 128)],
        [(PADDED, 128), (128, 128)],
        *fields, *coefs, source, weight,
    )
    halves = correct(first, everywhere(send), u, coefs, source)
    return jnp.concatenate(halves, axis=2)[0]


def solution(mesh):
    return jax.shard_map(
        body,
        mesh=mesh,
        in_specs=(P("gx", "gy", "gz"), P("gx", "gy", "gz")),
        out_specs=P("gx", "gy", "gz"),
        check_vma=False,
    )
```

```python
import functools

import jax
import jax.numpy as jnp
from jax import lax
from jax.experimental import pallas as pl
from jax.experimental.pallas import tpu as pltpu
from jax.sharding import PartitionSpec as P

SWEEPS = 4
CSWEEPS = 8
OMEGA = 0.8
KEEP = 0.2
AXES = ("gx", "gy", "gz")
NGX, NGY, NGZ = 8, 8, 4
BX, BY, BZ = 16, 16, 128
HALO = 8
PLANES = BZ + 2 * HALO
STEP = HALO * 8
ROWS = PLANES * 8
DEVICES = NGX * NGY * NGZ
F32 = jnp.float32
EXACT = lax.Precision.HIGHEST
VMEM_LIMIT = 24 * 1024 * 1024
BEFORE = ((1, 142, 2), (2, 140, 4), (3, 138, 3), (4, 136, 4))
AFTER = ((4, 136, 4), (6, 132, 4), (7, 130, 5), (8, 128, 4))


def call(kernel, outs, scratch, *args):
    return pl.pallas_call(
        kernel,
        out_shape=[jax.ShapeDtypeStruct(shape, F32) for shape in outs],
        in_specs=[pl.BlockSpec(memory_space=pltpu.VMEM)] * len(args),
        out_specs=[pl.BlockSpec(memory_space=pltpu.VMEM)] * len(outs),
        scratch_shapes=[pltpu.VMEM(shape, F32) for shape in scratch],
        compiler_params=pltpu.CompilerParams(vmem_limit_bytes=VMEM_LIMIT),
    )(*args)


def iota(dim, shape=(8, 128)):
    return lax.broadcasted_iota(jnp.int32, shape, dim)


def lanes(v, by):
    return pltpu.roll(v, by % 128, 1)


def subs(v, by):
    return pltpu.roll(v, by % 8, 0)


def east(v):
    turned = lanes(v, -32)
    return jnp.where(iota(1) < 96, turned, subs(turned, -1))


def west(v):
    turned = lanes(v, 32)
    return jnp.where(iota(1) >= 32, turned, subs(turned, 1))


def tile(ref, row):
    return ref[pl.ds(pl.multiple_of(row, 8), 8), :]


def put(ref, row, value):
    ref[pl.ds(pl.multiple_of(row, 8), 8), :] = value


def turns(start, count, times, step):
    per = count // times

    def body(n, _):
        step(pl.multiple_of((start + n * per) * 8, 8), per)
        return 0

    lax.fori_loop(0, times, body, 0)


def turn_kernel(count, own_lo, own_hi, y_lo, y_hi, x_lo, x_hi, out, z_lo, z_hi):
    for a in range(count):
        for sub in range(8):
            if sub < 2:
                block = x_lo[a, 4 * sub : 4 * sub + 4].reshape(128, 128)
            elif sub >= 6:
                block = x_hi[a, 4 * sub - 24 : 4 * sub - 20].reshape(128, 128)
            else:
                pieces = []
                for x in range(4 * sub - 8, 4 * sub - 4):
                    pieces += [y_lo[a, x], own_lo[a, x], own_hi[a, x], y_hi[a, x]]
                block = jnp.concatenate(pieces, axis=0)
            turned = block.T
            out[a, pl.ds(sub, BZ, stride=8), :] = turned
            z_lo[a, pl.ds(sub, HALO, stride=8), :] = turned[:HALO]
            z_hi[a, pl.ds(sub, HALO, stride=8), :] = turned[BZ - HALO :]


def turn(own_lo, own_hi, y_lo, y_hi, x_lo, x_hi):
    count = own_lo.shape[0]
    return call(
        functools.partial(turn_kernel, count),
        [(count, BZ * 8, 128), (count, STEP, 128), (count, STEP, 128)],
        [],
        own_lo, own_hi, y_lo, y_hi, x_lo, x_hi,
    )


def neighbours(before, here, after, coefs, row):
    hxm, hxp, hym, hyp, hzm, hzp = (tile(ref, row) for ref in coefs)
    total = (hzm * before + hzp * after) + (hxm * west(here) + hxp * east(here))
    return total + (hym * lanes(here, 1) + hyp * lanes(here, -1))


def walk(src, row, per, visit):
    before, here = tile(src, row - 8), tile(src, row)
    for n in range(per):
        after = tile(src, row + 8 * n + 8)
        visit(n, row + 8 * n, before, here, after)
        before, here = here, after


def sweep(src, dst, coefs, source, plan):
    def step(first, per):
        def visit(n, row, before, here, after):
            near = neighbours(before, here, after, coefs, row)
            put(dst, row, (KEEP * here + tile(source, row)) + near)

        walk(src, first, per, visit)

    turns(*plan, step)


def residual_layers(src, coefs, source, weight, layers):
    def step(first, per):
        sums = [None] * (per // 8)

        def visit(n, row, before, here, after):
            near = neighbours(before, here, after, coefs, row)
            rest = ((tile(source, row) - OMEGA * here) + near) * tile(weight, row)
            sums[n // 8] = rest if n % 8 == 0 else sums[n // 8] + rest
            if n % 8 == 7:
                put(layers, (first - STEP) // 8 + n - 7, sums[n // 8])

        walk(src, first, per, visit)

    turns(HALO, BZ, 4, step)


def coarse_pieces(layers):
    lane = iota(1, (16, 128)) % 32
    pieces = []
    for i in range(2):
        first = layers[pl.ds(2 + 2 * i, 16, stride=8), :]
        row = first + layers[pl.ds(3 + 2 * i, 16, stride=8), :]
        for j in range(2):
            pieces.append(jnp.where(lane // 8 == 1 + j, row, 0.0))
    return pieces


def send_rows(send, left, right):
    table = jnp.concatenate(left + right, axis=0)
    line = lax.dot_general(
        jnp.ones((8, 128), F32), table, (((1,), (1,)), ((), ())),
        precision=EXACT, preferred_element_type=F32,
    )
    send[...] = jnp.concatenate([line] * (DEVICES // 8), axis=0)


def places():
    gx, gy, gz = (lax.axis_index(name) for name in AXES)
    x = gx * BX - HALO + 4 * iota(0) + iota(1) // 32
    y = gy * BY - HALO + iota(1) % 32
    inside = (x >= 0) & (x < NGX * BX) & (y >= 0) & (y < NGY * BY)
    return inside, inside & (gz > 0), inside & (gz < NGZ - 1)


def fill(dst, own, low, high):
    inside, inside_low, inside_high = places()
    for n in range(HALO):
        put(dst, 8 * n, jnp.where(inside_low, tile(low, 8 * n), 0.0))
        put(dst, ROWS - STEP + 8 * n, jnp.where(inside_high, tile(high, 8 * n), 0.0))

    def step(first, per):
        for n in range(per):
            row = first + 8 * n
            put(dst, row, jnp.where(inside, tile(own, row - STEP), 0.0))

    turns(HALO, BZ, 4, step)


def first_kernel(
    own, z_lo, z_hi, hxm, hxp, hym, hyp, hzm, hzp, source, weight, u_out, send, cond, buf, layers, clayers
):
    fill(cond, own.at[1], z_lo.at[1], z_hi.at[1])
    inside, inside_low, inside_high = places()

    def coefs_of(first, per, here_mask, rhs, shift):
        def visit(n, row, before, c, after):
            fxm, fxp = c + west(c), c + east(c)
            fym, fyp = c + lanes(c, 1), c + lanes(c, -1)
            fzm, fzp = c + before, c + after
            diag = ((fxm + fxp) + (fym + fyp)) + (fzm + fzp)
            w = jnp.where(here_mask, OMEGA / jnp.where(here_mask, diag, 1.0), 0.0)
            for ref, face in zip((hxm, hxp, hym, hyp, hzm, hzp), (fxm, fxp, fym, fyp, fzm, fzp)):
                put(ref, row, w * face)
            g = (w + w) * tile(rhs, row - shift)
            put(source, row, g)
            put(weight, row, diag * (0.5 / OMEGA))
            put(buf, row, g)

        walk(cond, first, per, visit)

    coefs_of(8, HALO - 1, inside_low, z_lo.at[0], 0)
    coefs_of(ROWS - STEP, HALO - 1, inside_high, z_hi.at[0], ROWS - STEP)
    turns(HALO, BZ, 4, lambda first, per: coefs_of(first, per, inside, own.at[0], STEP))

    for n in range(16):
        clayers[pl.ds(8 * n, 8), :] = sum(tile(own.at[1], STEP * n + 8 * m) for m in range(8))

    coefs = (hxm, hxp, hym, hyp, hzm, hzp)
    sweep(buf, u_out, coefs, source, BEFORE[1])
    sweep(u_out, buf, coefs, source, BEFORE[2])
    sweep(buf, u_out, coefs, source, BEFORE[3])
    residual_layers(u_out, coefs, source, weight, layers)
    scaled = [piece * (1.0 / 64.0) for piece in coarse_pieces(clayers)]
    send_rows(send, coarse_pieces(layers), scaled)


def second_kernel(
    own, z_lo, z_hi, hxm, hxp, hym, hyp, hzm, hzp, source, weight, u_out, send, buf, layers
):
    fill(u_out, own.at[0], z_lo.at[0], z_hi.at[0])
    coefs = (hxm, hxp, hym, hyp, hzm, hzp)
    sweep(u_out, buf, coefs, source, BEFORE[0])
    sweep(buf, u_out, coefs, source, BEFORE[1])
    sweep(u_out, buf, coefs, source, BEFORE[2])
    sweep(buf, u_out, coefs, source, BEFORE[3])
    residual_layers(u_out, coefs, source, weight, layers)
    pieces = coarse_pieces(layers)
    send_rows(send, pieces, pieces)


KEYS = [(h, i, j, t) for h in range(2) for i in range(2) for j in range(2) for t in range(2)]


def coarse_tiles(half, table):
    out = {}
    for h, i, j, t in KEYS:
        row = half * 64 + i * 32 + j * 16 + t * 8
        out[h, i, j, t] = table[h][row : row + 8]
    return out


def coarse_neighbours(e):
    out = {}
    lane, sub = iota(1), iota(0)
    down = {key: subs(v, -1) for key, v in e.items()}
    up = {key: subs(v, 1) for key, v in e.items()}
    for h, i, j, t in KEYS:
        o = 1 - h
        if i == 0:
            turned = {n: lanes(e[n, 1, j, t], 32) for n in (0, 1)}
            xm = jnp.where(lane >= 32, turned[h], turned[o])
            xp = e[h, 1, j, t]
        else:
            turned = {n: lanes(e[n, 0, j, t], -32) for n in (0, 1)}
            xp = jnp.where(lane < 96, turned[h], turned[o])
            xm = e[h, 0, j, t]
        if j == 0:
            ym, yp = lanes(e[h, i, 1, t], 4), e[h, i, 1, t]
        else:
            ym, yp = e[h, i, 0, t], lanes(e[h, i, 0, t], -4)
        other_up, other_down = up[h, i, j, 1 - t], down[h, i, j, 1 - t]
        if t == 0:
            other_up = lanes(other_up, 1)
        else:
            other_down = lanes(other_down, -1)
        zm = jnp.where(sub > 0, up[h, i, j, t], other_up)
        zp = jnp.where(sub < 7, down[h, i, j, t], other_down)
        out[h, i, j, t] = (xm, xp, ym, yp, zm, zp)
    return out


def coarse_open(h, i, j, t):
    lane, sub = iota(1), iota(0)
    x = 2 * (4 * h + lane // 32) + i
    y = 2 * ((lane // 4) % 8) + j
    z = 16 * (lane % 4) + 8 * t + sub
    return x > 0, x < 2 * NGX - 1, y > 0, y < 2 * NGY - 1, z > 0, z < 16 * NGZ - 1


def coarse_solve(first, rhs, cc, cg, ext):
    table = [first[pl.ds(128 * h, 128), :].T for h in range(2)]
    cond = coarse_tiles(1, table)
    if rhs is not first:
        table = [rhs[pl.ds(128 * h, 128), :].T for h in range(2)]
    load = coarse_tiles(0, table)
    near = coarse_neighbours(cond)
    e = {}
    for n, key in enumerate(KEYS):
        open_sides = coarse_open(*key)
        faces = [cond[key] + jnp.where(o, v, 0.0) for o, v in zip(open_sides, near[key])]
        diag = ((faces[0] + faces[1]) + (faces[2] + faces[3])) + (faces[4] + faces[5])
        w = OMEGA / diag
        for m in range(6):
            cc[n, m] = jnp.where(open_sides[m], w * faces[m], 0.0)
        e[key] = (w + w) * load[key]
        cg[n] = e[key]

    def coarse_sweep(_, values):
        old = dict(zip(KEYS, values))
        near = coarse_neighbours(old)
        new = []
        for n, key in enumerate(KEYS):
            parts = [cc[n, m] * v for m, v in enumerate(near[key])]
            total = (parts[0] + parts[1]) + (parts[2] + parts[3])
            new.append((KEEP * old[key] + cg[n]) + total + (parts[4] + parts[5]))
        return new

    e = dict(zip(KEYS, lax.fori_loop(0, CSWEEPS - 1, coarse_sweep, [e[key] for key in KEYS])))
    sub = iota(0)
    for h, i, j, t in KEYS:
        if t == 0:
            low, high = subs(e[h, i, j, 0], 1), subs(e[h, i, j, 1], 1)
            at = 24 * (4 * h + 2 * i + j)
            ext[pl.ds(at, 8), :] = jnp.where(sub > 0, low, lanes(high, 1))
            ext[pl.ds(at + 8, 8), :] = jnp.where(sub > 0, high, low)
            ext[pl.ds(at + 16, 8), :] = jnp.where(sub == 0, high, lanes(low, -1))


def coarse_planes(ext, corr):
    gx, gy, gz = (lax.axis_index(name) for name in AXES)
    shape = (24, 128)
    part = (iota(1, shape) % 32) // 8
    y = 2 * gy - 1 + part
    z = 16 * gz - 1 + iota(0, shape)
    inside = (y >= 0) & (y < 2 * NGY) & (z >= 0) & (z < 16 * NGZ)
    sides = ((-1, 1), (0, 0), (0, 1), (1, 0))
    for n, (a, i) in enumerate(sides):
        px = (gx + a + NGX) % NGX
        valid = inside & (gx + a >= 0) & (gx + a < NGX)
        total = jnp.zeros(shape, F32)
        for m, (b, j) in enumerate(sides):
            py = (gy + b + NGY) % NGY
            lane = (px % 4) * 32 + py * 4 + gz
            at = pl.multiple_of(24 * (4 * (px // 4) + 2 * i + j), 8)
            near = pltpu.roll(ext[pl.ds(at, 24), :], (128 - lane) % 128, 1)
            total = jnp.where(part == m, jnp.broadcast_to(near[:, :1], shape), total)
        total = jnp.where(valid, total, 0.0)
        corr[pl.ds(2 * n, 24, stride=8), :] = total
        corr[pl.ds(2 * n + 1, 24, stride=8), :] = total


def correct_kernel(
    split, first, rhs, u, hxm, hxp, hym, hyp, hzm, hzp, source, *rest
):
    outs, (buf, other, cc, cg, ext, corr) = rest[: 1 + split], rest[1 + split :]
    coarse_solve(first, first if split else rhs, cc, cg, ext)
    coarse_planes(ext, corr)
    for t in range(PLANES // 8):
        layer = tile(corr, 8 * t)
        for plane in range(max(8 * t, 3), min(8 * t + 8, PLANES - 3)):
            put(buf, 8 * plane, tile(u, 8 * plane) + layer)
    coefs = (hxm, hxp, hym, hyp, hzm, hzp)
    sweep(buf, other, coefs, source, AFTER[0])
    sweep(other, buf, coefs, source, AFTER[1])
    sweep(buf, other, coefs, source, AFTER[2])
    sweep(other, buf, coefs, source, AFTER[3])
    for sub in range(2, 6):
        block = buf[pl.ds(STEP + sub, BZ, stride=8), :].T
        for g in range(4):
            x = 4 * sub - 8 + g
            own = block[32 * g + 8 : 32 * g + 24]
            if split:
                outs[0][0, x] = own[:8]
                outs[1][0, x] = own[8:]
            else:
                outs[0][x] = own


def ring(value, axis, size, by):
    return lax.ppermute(value, axis, [(n, (n + by) % size) for n in range(size)])


def from_both(low, high, axis, size):
    return ring(high, axis, size, 1), ring(low, axis, size, -1)


def spread_planes(own_lo, own_hi):
    y_lo, y_hi = from_both(own_lo, own_hi, "gy", NGY)
    lows = [part[:, :8] for part in (y_lo, own_lo, own_hi, y_hi)]
    highs = [part[:, 8:] for part in (y_lo, own_lo, own_hi, y_hi)]
    x_lo, x_hi = from_both(
        jnp.concatenate(lows, axis=2), jnp.concatenate(highs, axis=2), "gx", NGX
    )
    own, z_lo, z_hi = turn(own_lo, own_hi, y_lo, y_hi, x_lo, x_hi)
    return (own, *from_both(z_lo, z_hi, "gz", NGZ))


def everywhere(send):
    return lax.all_to_all(send, AXES, 0, 0, tiled=True)


def correct(split, first, rhs, u, coefs, source):
    return call(
        functools.partial(correct_kernel, split),
        [(1, BX, 8, 128)] * 2 if split else [(BX, BY, BZ)],
        [(ROWS, 128), (ROWS, 128), (16, 6, 8, 128), (16, 8, 128), (8 * 24, 128), (24 * 8, 128)],
        first, rhs, u, *coefs, source,
    )


def body(right_side, conductivity):
    both = jnp.stack([right_side, conductivity])
    fields = spread_planes(both[:, :, :8], both[:, :, 8:])
    *coefs, source, weight, u, send = call(
        first_kernel,
        [(ROWS, 128)] * 9 + [(DEVICES, 128)],
        [(ROWS, 128), (ROWS, 128), (128, 128), (128, 128)],
        *fields,
    )
    first = everywhere(send)
    halves = correct(True, first, first, u, coefs, source)
    u, send = call(
        second_kernel,
        [(ROWS, 128), (DEVICES, 128)],
        [(ROWS, 128), (128, 128)],
        *spread_planes(*halves), *coefs, source, weight,
    )
    return correct(False, first, everywhere(send), u, coefs, source)[0]


def solution(mesh):
    return jax.shard_map(
        body,
        mesh=mesh,
        in_specs=(P("gx", "gy", "gz"), P("gx", "gy", "gz")),
        out_specs=P("gx", "gy", "gz"),
        check_vma=False,
    )
```

```python
import functools

import jax
import jax.numpy as jnp
from jax import lax
from jax.experimental import pallas as pl
from jax.experimental.pallas import tpu as pltpu
from jax.sharding import PartitionSpec as P

SWEEPS = 4
CSWEEPS = 8
OMEGA = 0.8
KEEP = 0.2
AXES = ("gx", "gy", "gz")
NGX, NGY, NGZ = 8, 8, 4
BX, BY, BZ = 16, 16, 128
HALO = 8
PLANES = BZ + 2 * HALO
STEP = HALO * 8
ROWS = PLANES * 8
DEVICES = NGX * NGY * NGZ
F32 = jnp.float32
EXACT = lax.Precision.HIGHEST
VMEM_LIMIT = 24 * 1024 * 1024
COST = 8_000_000
AFTER = ((4, 136, 4), (6, 132, 4), (7, 130, 5), (8, 128, 4))
INNER = ((9, 126, 3), (10, 124, 4), (11, 122, 2), (12, 120, 3))


def call(kernel, outs, scratch, *args, aliases={}, cost=None):
    if cost is not None:
        cost = pl.CostEstimate(flops=cost, bytes_accessed=cost, transcendentals=0)
    return pl.pallas_call(
        kernel,
        out_shape=[jax.ShapeDtypeStruct(shape, F32) for shape in outs],
        in_specs=[pl.BlockSpec(memory_space=pltpu.VMEM)] * len(args),
        out_specs=[pl.BlockSpec(memory_space=pltpu.VMEM)] * len(outs),
        scratch_shapes=[pltpu.VMEM(shape, F32) for shape in scratch],
        input_output_aliases=aliases,
        cost_estimate=cost,
        compiler_params=pltpu.CompilerParams(vmem_limit_bytes=VMEM_LIMIT),
    )(*args)


def iota(dim, shape=(8, 128)):
    return lax.broadcasted_iota(jnp.int32, shape, dim)


def lanes(v, by):
    return pltpu.roll(v, by % 128, 1)


def subs(v, by):
    return pltpu.roll(v, by % 8, 0)


def east(v):
    turned = subs(v, -1)
    return jnp.where(iota(0) < 7, turned, lanes(turned, -32))


def west(v):
    turned = subs(v, 1)
    return jnp.where(iota(0) > 0, turned, lanes(turned, 32))


def tile(ref, row):
    return ref[pl.ds(pl.multiple_of(row, 8), 8), :]


def put(ref, row, value):
    ref[pl.ds(pl.multiple_of(row, 8), 8), :] = value


def turns(start, count, times, step):
    per = count // times

    def body(n, _):
        step(pl.multiple_of((start + n * per) * 8, 8), per)
        return 0

    lax.fori_loop(0, times, body, 0)


def place(sub):
    gx, gy = (lax.axis_index(name) for name in AXES[:2])
    lane = iota(1, sub.shape)
    x = gx * BX - HALO + 8 * (lane // 32) + sub
    y = gy * BY - HALO + lane % 32
    return (x >= 0) & (x < NGX * BX) & (y >= 0) & (y < NGY * BY)


def turn_kernel(count, own_lo, own_hi, y_lo, y_hi, x_lo, x_hi, out, z_lo, z_hi):
    for sub in range(8):
        inside = place(jnp.full((BZ, 128), sub, jnp.int32))
        for a in range(count):
            pieces = [x_lo[a, sub]]
            for x in (sub, 8 + sub):
                pieces += [y_lo[a, x], own_lo[a, x], own_hi[a, x], y_hi[a, x]]
            pieces += [x_hi[a, sub]]
            turned = jnp.where(inside, jnp.concatenate(pieces, axis=0).T, 0.0)
            out[a, pl.ds(STEP + sub, BZ, stride=8), :] = turned
            z_lo[a, pl.ds(sub, HALO, stride=8), :] = turned[:HALO]
            z_hi[a, pl.ds(sub, HALO, stride=8), :] = turned[BZ - HALO :]


def turn(own_lo, own_hi, y_lo, y_hi, x_lo, x_hi):
    count = own_lo.shape[0]
    return call(
        functools.partial(turn_kernel, count),
        [(count, ROWS, 128), (count, STEP, 128), (count, STEP, 128)],
        [],
        own_lo, own_hi, y_lo, y_hi, x_lo, x_hi,
    )


def walk(src, first, per, visit):
    before, here = tile(src, first - 8), tile(src, first)
    base = None
    for n in range(per):
        if base is None or n >= base + 8:
            base = min(n, per - 8)
            start = pl.multiple_of(first + 8 * base, 8)
            ahead = lanes(src[pl.ds(start, 8, stride=8), :], -32)
            behind = lanes(src[pl.ds(start + 7, 8, stride=8), :], 32)
        after = tile(src, first + 8 * n + 8)
        xp = jnp.where(iota(0) < 7, subs(here, -1), subs(ahead, 7 - (n - base)))
        xm = jnp.where(iota(0) > 0, subs(here, 1), subs(behind, -(n - base)))
        visit(n, first + 8 * n, here, (xm, xp, lanes(here, 1), lanes(here, -1), before, after))
        before, here = here, after


def weighted(coefs, near):
    parts = [c * v for c, v in zip(coefs, near)]
    return ((parts[4] + parts[5]) + (parts[0] + parts[1])) + (parts[2] + parts[3])


def renewed(here, g, coefs, near):
    return (KEEP * here + g) + weighted(coefs, near)


def remaining(here, g, weight, coefs, near):
    return ((g - OMEGA * here) + weighted(coefs, near)) * weight


def sweep(src, dst, coefs, source, plan):
    def step(first, per):
        def visit(n, row, here, near):
            put(dst, row, renewed(here, tile(source, row), [tile(ref, row) for ref in coefs], near))

        walk(src, first, per, visit)

    turns(*plan, step)


def residual_layers(src, coefs, source, weight, layers):
    def step(first, per):
        sums = [None]

        def visit(n, row, here, near):
            rest = remaining(
                here, tile(source, row), tile(weight, row), [tile(ref, row) for ref in coefs], near
            )
            sums[0] = rest if n % 8 == 0 else sums[0] + rest
            if n % 8 == 7:
                put(layers, (first - STEP) // 8 + n - 7, sums[0])

        walk(src, first, per, visit)

    turns(16, 112, 2, step)


def coarse_pieces(layers):
    lane = iota(1, (16, 128))
    rows = [layers[pl.ds(sub, 16, stride=8), :] for sub in range(8)]
    row = ((rows[0] + rows[1]) + (rows[2] + rows[3])) + ((rows[4] + rows[5]) + (rows[6] + rows[7]))
    return [jnp.where(lane // 8 == 5 + 4 * i + j, row, 0.0) for i in range(2) for j in range(2)]


def send_rows(send, left, right):
    table = jnp.concatenate(left + right, axis=0)
    line = lax.dot_general(
        jnp.ones((8, 128), F32), table, (((1,), (1,)), ((), ())),
        precision=EXACT, preferred_element_type=F32,
    )
    send[...] = jnp.concatenate([line] * (DEVICES // 8), axis=0)


def coefs_at(inside, c, near, rhs):
    faces = [c + v for v in near]
    diag = ((faces[0] + faces[1]) + (faces[2] + faces[3])) + (faces[4] + faces[5])
    w = jnp.where(inside, OMEGA / jnp.where(inside, diag, 1.0), 0.0)
    return [w * face for face in faces], (w + w) * rhs, diag * (0.5 / OMEGA)


def inner_kernel(
    own, hxm, hxp, hym, hyp, hzm, hzp, source, weight, u1, u2, u3, u4, layers, clayers
):
    coefs = (hxm, hxp, hym, hyp, hzm, hzp)
    inside = place(iota(0))

    def coefs_of(first, per):
        def visit(n, row, c, near):
            held, g, rest = coefs_at(inside, c, near, tile(own.at[0], row))
            for ref, value in zip(coefs, held):
                put(ref, row, value)
            put(source, row, g)
            put(weight, row, rest)
            put(u1, row, g)

        walk(own.at[1], first, per, visit)

    turns(*INNER[0], coefs_of)
    for n in range(16):
        put(clayers, 8 * n, sum(tile(own.at[1], STEP + STEP * n + 8 * m) for m in range(8)))
    sweep(u1, u2, coefs, source, INNER[1])
    sweep(u2, u3, coefs, source, INNER[2])
    sweep(u3, u4, coefs, source, INNER[3])
    residual_layers(u4, coefs, source, weight, layers)


def inner_again_kernel(
    own, hxm, hxp, hym, hyp, hzm, hzp, source, weight, u1, u2, u3, u4, layers
):
    coefs = (hxm, hxp, hym, hyp, hzm, hzp)
    sweep(own.at[0], u1, coefs, source, INNER[0])
    sweep(u1, u2, coefs, source, INNER[1])
    sweep(u2, u3, coefs, source, INNER[2])
    sweep(u3, u4, coefs, source, INNER[3])
    residual_layers(u4, coefs, source, weight, layers)


def ends(first, count=8):
    return list(range(first, first + count)), list(range(PLANES - first - count, PLANES - first))


def around(get, p):
    here = get(p)
    return here, (west(here), east(here), lanes(here, 1), lanes(here, -1), get(p - 1), get(p + 1))


def finish(own, z_lo, z_hi):
    gz = lax.axis_index("gz")

    def get(p):
        if p < HALO:
            return jnp.where(gz > 0, tile(z_lo, 8 * p), 0.0)
        if p >= PLANES - HALO:
            return jnp.where(gz < NGZ - 1, tile(z_hi, 8 * (p - PLANES + HALO)), 0.0)
        return tile(own, 8 * p)

    return get


def known(values, ref):
    return lambda p: values[p] if p in values else tile(ref, 8 * p)


def end_sweeps(get, refs, first, coefs_of, g_of):
    for n, ref in enumerate(refs):
        values = {}
        for p in sum(ends(first + n), []):
            here, near = around(get, p)
            values[p] = renewed(here, g_of(p), coefs_of(p), near)
        get = known(values, ref)
    return get, values


def end_layers(get, layers, coefs_of, g_of, weight_of):
    sums = []
    for planes in ends(8):
        parts = []
        for p in planes:
            here, near = around(get, p)
            parts.append(remaining(here, g_of(p), weight_of(p), coefs_of(p), near))
        sums.append(sum(parts[1:], parts[0]))
    put(layers, 0, sums[0])
    put(layers, 120, sums[1])


def ends_kernel(
    own, z_lo, z_hi, u1, u2, u3, inner, clayers, *rest
):
    held, (new, send, layers) = rest[:9], (rest[9:18], rest[18], rest[19])
    gz = lax.axis_index("gz")
    inside = place(iota(0))
    low, high = inside & (gz > 0), inside & (gz < NGZ - 1)
    cond, rhs = finish(own.at[1], z_lo.at[1], z_hi.at[1]), finish(own.at[0], z_lo.at[0], z_hi.at[0])
    table = {}
    for p in sum(ends(1), []):
        mask = low if p < HALO else high if p >= PLANES - HALO else inside
        c, near = around(cond, p)
        table[p] = coefs_at(mask, c, near, rhs(p))
        for ref, value in zip(new, (*table[p][0], *table[p][1:])):
            put(ref, 8 * p, value)

    def coefs_of(p):
        return table[p][0] if p in table else [tile(ref, 8 * p) for ref in held[:6]]

    def g_of(p):
        return table[p][1] if p in table else tile(held[6], 8 * p)

    def weight_of(p):
        return table[p][2] if p in table else tile(held[7], 8 * p)

    start = known({p: entry[1] for p, entry in table.items()}, u1)
    get, values = end_sweeps(start, (u2, u3, held[8]), 2, coefs_of, g_of)
    for p, value in values.items():
        put(new[8], 8 * p, value)
    for n in range(1, 15):
        put(layers, 8 * n, tile(inner, 8 * n))
    end_layers(get, layers, coefs_of, g_of, weight_of)
    scaled = [piece * (1.0 / 64.0) for piece in coarse_pieces(clayers)]
    send_rows(send, coarse_pieces(layers), scaled)


def ends_again_kernel(
    own, z_lo, z_hi, u1, u2, u3, inner, hxm, hxp, hym, hyp, hzm, hzp, source, weight, u4, new, send, layers
):
    def coefs_of(p):
        return [tile(ref, 8 * p) for ref in (hxm, hxp, hym, hyp, hzm, hzp)]

    def g_of(p):
        return tile(source, 8 * p)

    def weight_of(p):
        return tile(weight, 8 * p)

    start = finish(own.at[0], z_lo.at[0], z_hi.at[0])
    get, values = end_sweeps(start, (u1, u2, u3, u4), 1, coefs_of, g_of)
    for p, value in values.items():
        put(new, 8 * p, value)
    for n in range(1, 15):
        put(layers, 8 * n, tile(inner, 8 * n))
    end_layers(get, layers, coefs_of, g_of, weight_of)
    pieces = coarse_pieces(layers)
    send_rows(send, pieces, pieces)


KEYS = [(h, i, j, t) for h in range(2) for i in range(2) for j in range(2) for t in range(2)]


def coarse_tiles(half, table):
    out = {}
    for h, i, j, t in KEYS:
        row = half * 64 + i * 32 + j * 16 + t * 8
        out[h, i, j, t] = table[h][row : row + 8]
    return out


def coarse_neighbours(e):
    out = {}
    lane, sub = iota(1), iota(0)
    down = {key: subs(v, -1) for key, v in e.items()}
    up = {key: subs(v, 1) for key, v in e.items()}
    for h, i, j, t in KEYS:
        o = 1 - h
        if i == 0:
            turned = {n: lanes(e[n, 1, j, t], 32) for n in (0, 1)}
            xm = jnp.where(lane >= 32, turned[h], turned[o])
            xp = e[h, 1, j, t]
        else:
            turned = {n: lanes(e[n, 0, j, t], -32) for n in (0, 1)}
            xp = jnp.where(lane < 96, turned[h], turned[o])
            xm = e[h, 0, j, t]
        if j == 0:
            ym, yp = lanes(e[h, i, 1, t], 4), e[h, i, 1, t]
        else:
            ym, yp = e[h, i, 0, t], lanes(e[h, i, 0, t], -4)
        other_up, other_down = up[h, i, j, 1 - t], down[h, i, j, 1 - t]
        if t == 0:
            other_up = lanes(other_up, 1)
        else:
            other_down = lanes(other_down, -1)
        zm = jnp.where(sub > 0, up[h, i, j, t], other_up)
        zp = jnp.where(sub < 7, down[h, i, j, t], other_down)
        out[h, i, j, t] = (xm, xp, ym, yp, zm, zp)
    return out


def coarse_open(h, i, j, t):
    lane, sub = iota(1), iota(0)
    x = 2 * (4 * h + lane // 32) + i
    y = 2 * ((lane // 4) % 8) + j
    z = 16 * (lane % 4) + 8 * t + sub
    return x > 0, x < 2 * NGX - 1, y > 0, y < 2 * NGY - 1, z > 0, z < 16 * NGZ - 1


def coarse_solve(first, rhs, cc, cg, ext):
    table = [first[pl.ds(128 * h, 128), :].T for h in range(2)]
    cond = coarse_tiles(1, table)
    if rhs is not first:
        table = [rhs[pl.ds(128 * h, 128), :].T for h in range(2)]
    load = coarse_tiles(0, table)
    near = coarse_neighbours(cond)
    e = {}
    for n, key in enumerate(KEYS):
        open_sides = coarse_open(*key)
        faces = [cond[key] + jnp.where(o, v, 0.0) for o, v in zip(open_sides, near[key])]
        diag = ((faces[0] + faces[1]) + (faces[2] + faces[3])) + (faces[4] + faces[5])
        w = OMEGA / diag
        for m in range(6):
            cc[n, m] = jnp.where(open_sides[m], w * faces[m], 0.0)
        e[key] = (w + w) * load[key]
        cg[n] = e[key]

    def coarse_sweep(_, values):
        old = dict(zip(KEYS, values))
        near = coarse_neighbours(old)
        new = []
        for n, key in enumerate(KEYS):
            parts = [cc[n, m] * v for m, v in enumerate(near[key])]
            total = (parts[0] + parts[1]) + (parts[2] + parts[3])
            new.append((KEEP * old[key] + cg[n]) + total + (parts[4] + parts[5]))
        return new

    e = dict(zip(KEYS, lax.fori_loop(0, CSWEEPS - 1, coarse_sweep, [e[key] for key in KEYS])))
    sub = iota(0)
    for h, i, j, t in KEYS:
        if t == 0:
            low, high = subs(e[h, i, j, 0], 1), subs(e[h, i, j, 1], 1)
            at = 24 * (4 * h + 2 * i + j)
            ext[pl.ds(at, 8), :] = jnp.where(sub > 0, low, lanes(high, 1))
            ext[pl.ds(at + 8, 8), :] = jnp.where(sub > 0, high, low)
            ext[pl.ds(at + 16, 8), :] = jnp.where(sub == 0, high, lanes(low, -1))


def coarse_lines(ext):
    gx, gy, gz = (lax.axis_index(name) for name in AXES)
    shape = (24, 128)
    part = iota(1, shape) // 8
    x = 2 * gx - 1 + part // 4
    y = 2 * gy - 1 + part % 4
    z = 16 * gz - 1 + iota(0, shape)
    inside = (x >= 0) & (x < 2 * NGX) & (y >= 0) & (y < 2 * NGY) & (z >= 0) & (z < 16 * NGZ)
    sides = ((-1, 1), (0, 0), (0, 1), (1, 0))
    total = jnp.zeros(shape, F32)
    for n, (a, i) in enumerate(sides):
        px = (gx + a + NGX) % NGX
        for m, (b, j) in enumerate(sides):
            py = (gy + b + NGY) % NGY
            lane = (px % 4) * 32 + py * 4 + gz
            at = pl.multiple_of(24 * (4 * (px // 4) + 2 * i + j), 8)
            near = pltpu.roll(ext[pl.ds(at, 24), :], (128 - lane) % 128, 1)
            total = jnp.where(part == 4 * n + m, jnp.broadcast_to(near[:, :1], shape), total)
    return jnp.where(inside, total, 0.0)


def correct_kernel(
    split, first, rhs, u, hxm, hxp, hym, hyp, hzm, hzp, source, *rest
):
    outs, (buf, other, cc, cg, ext) = rest[: 1 + split], rest[1 + split :]
    coarse_solve(first, first if split else rhs, cc, cg, ext)
    lines = coarse_lines(ext)
    for t in range(PLANES // 8):
        layer = jnp.broadcast_to(lines[t : t + 1], (8, 128))
        for plane in range(max(8 * t, 4), min(8 * t + 8, PLANES - 4)):
            put(buf, 8 * plane, tile(u, 8 * plane) + layer)
    for plane in (3, PLANES - 4):
        put(buf, 8 * plane, jnp.zeros((8, 128), F32))
    coefs = (hxm, hxp, hym, hyp, hzm, hzp)
    sweep(buf, other, coefs, source, AFTER[0])
    sweep(other, buf, coefs, source, AFTER[1])
    sweep(buf, other, coefs, source, AFTER[2])
    sweep(other, buf, coefs, source, AFTER[3])
    for sub in range(8):
        block = buf[pl.ds(STEP + sub, BZ, stride=8), :].T
        for g in (1, 2):
            x = 8 * g - 8 + sub
            own = block[32 * g + 8 : 32 * g + 24]
            if split:
                outs[0][0, x] = own[:8]
                outs[1][0, x] = own[8:]
            else:
                outs[0][x] = own


def ring(value, axis, size, by):
    return lax.ppermute(value, axis, [(n, (n + by) % size) for n in range(size)])


def from_both(low, high, axis, size):
    return ring(high, axis, size, 1), ring(low, axis, size, -1)


def spread_planes(own_lo, own_hi):
    y_lo, y_hi = from_both(own_lo, own_hi, "gy", NGY)
    lows = [part[:, :8] for part in (y_lo, own_lo, own_hi, y_hi)]
    highs = [part[:, 8:] for part in (y_lo, own_lo, own_hi, y_hi)]
    x_lo, x_hi = from_both(
        jnp.concatenate(lows, axis=2), jnp.concatenate(highs, axis=2), "gx", NGX
    )
    own, z_lo, z_hi = turn(own_lo, own_hi, y_lo, y_hi, x_lo, x_hi)
    return (own, *from_both(z_lo, z_hi, "gz", NGZ))


def everywhere(send):
    return lax.all_to_all(send, AXES, 0, 0, tiled=True)


def correct(split, first, rhs, u, coefs, source):
    return call(
        functools.partial(correct_kernel, split),
        [(1, BX, 8, 128)] * 2 if split else [(BX, BY, BZ)],
        [(ROWS, 128), (ROWS, 128), (16, 6, 8, 128), (16, 8, 128), (8 * 24, 128)],
        first, rhs, u, *coefs, source,
    )


def body(right_side, conductivity):
    both = jnp.stack([right_side, conductivity])
    own, z_lo, z_hi = spread_planes(both[:, :, :8], both[:, :, 8:])
    *held, u1, u2, u3, u4, layers, clayers = call(
        inner_kernel, [(ROWS, 128)] * 12 + [(128, 128)] * 2, [], own, cost=COST
    )
    *coefs, source, weight, u, send = call(
        ends_kernel,
        [(ROWS, 128)] * 9 + [(DEVICES, 128)],
        [(128, 128)],
        own, z_lo, z_hi, u1, u2, u3, layers, clayers, *held, u4,
        aliases={8 + n: n for n in range(9)},
    )
    first = everywhere(send)
    halves = correct(True, first, first, u, coefs, source)
    own, z_lo, z_hi = spread_planes(*halves)
    u1, u2, u3, u4, layers = call(
        inner_again_kernel,
        [(ROWS, 128)] * 4 + [(128, 128)],
        [],
        own, *coefs, source, weight, cost=COST,
    )
    u, send = call(
        ends_again_kernel,
        [(ROWS, 128), (DEVICES, 128)],
        [(128, 128)],
        own, z_lo, z_hi, u1, u2, u3, layers, *coefs, source, weight, u4,
        aliases={15: 0},
    )
    return correct(False, first, everywhere(send), u, coefs, source)[0]


def solution(mesh):
    return jax.shard_map(
        body,
        mesh=mesh,
        in_specs=(P("gx", "gy", "gz"), P("gx", "gy", "gz")),
        out_specs=P("gx", "gy", "gz"),
        check_vma=False,
    )
```

```python
import functools

import jax
import jax.numpy as jnp
from jax import lax
from jax.experimental import pallas as pl
from jax.experimental.pallas import tpu as pltpu
from jax.sharding import PartitionSpec as P

SWEEPS = 4
CSWEEPS = 8
OMEGA = 0.8
KEEP = 0.2
AXES = ("gx", "gy", "gz")
NGX, NGY, NGZ = 8, 8, 4
BX, BY, BZ = 16, 16, 128
HALO = 8
PLANES = BZ + 2 * HALO
STEP = HALO * 8
ROWS = PLANES * 8
DEVICES = NGX * NGY * NGZ
F32 = jnp.float32
EXACT = lax.Precision.HIGHEST
VMEM_LIMIT = 24 * 1024 * 1024
COST = 8_000_000
AFTER = ((4, 136, 1), (6, 132, 1), (7, 130, 1), (8, 128, 1))
INNER = ((9, 126, 3), (10, 124, 4), (11, 122, 2), (12, 120, 3))


def call(kernel, outs, scratch, *args, aliases={}, cost=None):
    if cost is not None:
        cost = pl.CostEstimate(flops=cost, bytes_accessed=cost, transcendentals=0)
    return pl.pallas_call(
        kernel,
        out_shape=[jax.ShapeDtypeStruct(shape, F32) for shape in outs],
        in_specs=[pl.BlockSpec(memory_space=pltpu.VMEM)] * len(args),
        out_specs=[pl.BlockSpec(memory_space=pltpu.VMEM)] * len(outs),
        scratch_shapes=[pltpu.VMEM(shape, F32) for shape in scratch],
        input_output_aliases=aliases,
        cost_estimate=cost,
        compiler_params=pltpu.CompilerParams(vmem_limit_bytes=VMEM_LIMIT),
    )(*args)


def iota(dim, shape=(8, 128)):
    return lax.broadcasted_iota(jnp.int32, shape, dim)


def lanes(v, by):
    return pltpu.roll(v, by % 128, 1)


def subs(v, by):
    return pltpu.roll(v, by % 8, 0)


def east(v):
    turned = subs(v, -1)
    return jnp.where(iota(0) < 7, turned, lanes(turned, -32))


def west(v):
    turned = subs(v, 1)
    return jnp.where(iota(0) > 0, turned, lanes(turned, 32))


def tile(ref, row):
    return ref[pl.ds(pl.multiple_of(row, 8), 8), :]


def put(ref, row, value):
    ref[pl.ds(pl.multiple_of(row, 8), 8), :] = value


def turns(start, count, times, step):
    per = count // times
    rims = iota(0) > 0, iota(0) < 7

    def body(n, _):
        step(pl.multiple_of((start + n * per) * 8, 8), per, rims)
        return 0

    lax.fori_loop(0, times, body, 0)


def place(sub):
    gx, gy = (lax.axis_index(name) for name in AXES[:2])
    lane = iota(1, sub.shape)
    x = gx * BX - HALO + 8 * (lane // 32) + sub
    y = gy * BY - HALO + lane % 32
    return (x >= 0) & (x < NGX * BX) & (y >= 0) & (y < NGY * BY)


def turn_kernel(count, own_lo, own_hi, y_lo, y_hi, x_lo, x_hi, out, z_lo, z_hi):
    for sub in range(8):
        inside = place(jnp.full((BZ, 128), sub, jnp.int32))
        for a in range(count):
            pieces = [x_lo[a, sub]]
            for x in (sub, 8 + sub):
                pieces += [y_lo[a, x], own_lo[a, x], own_hi[a, x], y_hi[a, x]]
            pieces += [x_hi[a, sub]]
            turned = jnp.where(inside, jnp.concatenate(pieces, axis=0).T, 0.0)
            out[a, pl.ds(STEP + sub, BZ, stride=8), :] = turned
            z_lo[a, pl.ds(sub, HALO, stride=8), :] = turned[:HALO]
            z_hi[a, pl.ds(sub, HALO, stride=8), :] = turned[BZ - HALO :]


def turn(own_lo, own_hi, y_lo, y_hi, x_lo, x_hi):
    count = own_lo.shape[0]
    return call(
        functools.partial(turn_kernel, count),
        [(count, ROWS, 128), (count, STEP, 128), (count, STEP, 128)],
        [],
        own_lo, own_hi, y_lo, y_hi, x_lo, x_hi,
    )


def walk(src, first, per, rims, visit):
    not_first, not_last = rims
    before, here = tile(src, first - 8), tile(src, first)
    base = None
    for n in range(per):
        if base is None or n >= base + 8:
            base = min(n, per - 8)
            start = pl.multiple_of(first + 8 * base, 8)
            ahead = lanes(src[pl.ds(start, 8, stride=8), :], -32)
            behind = lanes(src[pl.ds(start + 7, 8, stride=8), :], 32)
        after = tile(src, first + 8 * n + 8)
        xp = jnp.where(not_last, subs(here, -1), subs(ahead, 7 - (n - base)))
        xm = jnp.where(not_first, subs(here, 1), subs(behind, -(n - base)))
        visit(n, first + 8 * n, here, (xm, xp, lanes(here, 1), lanes(here, -1), before, after))
        before, here = here, after


def weighted(coefs, near):
    parts = [c * v for c, v in zip(coefs, near)]
    return ((parts[4] + parts[5]) + (parts[0] + parts[1])) + (parts[2] + parts[3])


def renewed(here, g, coefs, near):
    return (KEEP * here + g) + weighted(coefs, near)


def remaining(here, g, weight, coefs, near):
    return ((g - OMEGA * here) + weighted(coefs, near)) * weight


def sweep(src, dst, coefs, source, plan):
    def step(first, per, rims):
        def visit(n, row, here, near):
            put(dst, row, renewed(here, tile(source, row), [tile(ref, row) for ref in coefs], near))

        walk(src, first, per, rims, visit)

    turns(*plan, step)


def residual_layers(src, coefs, source, weight, layers):
    def step(first, per, rims):
        sums = [None]

        def visit(n, row, here, near):
            rest = remaining(
                here, tile(source, row), tile(weight, row), [tile(ref, row) for ref in coefs], near
            )
            sums[0] = rest if n % 8 == 0 else sums[0] + rest
            if n % 8 == 7:
                put(layers, (first - STEP) // 8 + n - 7, sums[0])

        walk(src, first, per, rims, visit)

    turns(16, 112, 2, step)


def coarse_pieces(layers):
    lane = iota(1, (16, 128))
    rows = [layers[pl.ds(sub, 16, stride=8), :] for sub in range(8)]
    row = ((rows[0] + rows[1]) + (rows[2] + rows[3])) + ((rows[4] + rows[5]) + (rows[6] + rows[7]))
    return [jnp.where(lane // 8 == 5 + 4 * i + j, row, 0.0) for i in range(2) for j in range(2)]


def send_rows(send, left, right):
    table = jnp.concatenate(left + right, axis=0)
    line = lax.dot_general(
        jnp.ones((8, 128), F32), table, (((1,), (1,)), ((), ())),
        precision=EXACT, preferred_element_type=F32,
    )
    send[...] = jnp.concatenate([line] * (DEVICES // 8), axis=0)


def coefs_at(inside, c, near, rhs):
    faces = [c + v for v in near]
    diag = ((faces[0] + faces[1]) + (faces[2] + faces[3])) + (faces[4] + faces[5])
    w = jnp.where(inside, OMEGA / jnp.where(inside, diag, 1.0), 0.0)
    return [w * face for face in faces], (w + w) * rhs, diag * (0.5 / OMEGA)


def inner_kernel(
    own, hxm, hxp, hym, hyp, hzm, hzp, source, weight, u1, u2, u3, u4, layers, clayers
):
    coefs = (hxm, hxp, hym, hyp, hzm, hzp)
    inside = place(iota(0))

    def coefs_of(first, per, rims):
        def visit(n, row, c, near):
            held, g, rest = coefs_at(inside, c, near, tile(own.at[0], row))
            for ref, value in zip(coefs, held):
                put(ref, row, value)
            put(source, row, g)
            put(weight, row, rest)
            put(u1, row, g)

        walk(own.at[1], first, per, rims, visit)

    turns(*INNER[0], coefs_of)
    for n in range(16):
        put(clayers, 8 * n, sum(tile(own.at[1], STEP + STEP * n + 8 * m) for m in range(8)))
    sweep(u1, u2, coefs, source, INNER[1])
    sweep(u2, u3, coefs, source, INNER[2])
    sweep(u3, u4, coefs, source, INNER[3])
    residual_layers(u4, coefs, source, weight, layers)


def inner_again_kernel(
    own, hxm, hxp, hym, hyp, hzm, hzp, source, weight, u1, u2, u3, u4, layers
):
    coefs = (hxm, hxp, hym, hyp, hzm, hzp)
    sweep(own.at[0], u1, coefs, source, INNER[0])
    sweep(u1, u2, coefs, source, INNER[1])
    sweep(u2, u3, coefs, source, INNER[2])
    sweep(u3, u4, coefs, source, INNER[3])
    residual_layers(u4, coefs, source, weight, layers)


def ends(first, count=8):
    return list(range(first, first + count)), list(range(PLANES - first - count, PLANES - first))


def around(get, p):
    here = get(p)
    return here, (west(here), east(here), lanes(here, 1), lanes(here, -1), get(p - 1), get(p + 1))


def finish(own, z_lo, z_hi):
    gz = lax.axis_index("gz")

    def get(p):
        if p < HALO:
            return jnp.where(gz > 0, tile(z_lo, 8 * p), 0.0)
        if p >= PLANES - HALO:
            return jnp.where(gz < NGZ - 1, tile(z_hi, 8 * (p - PLANES + HALO)), 0.0)
        return tile(own, 8 * p)

    return get


def known(values, ref):
    return lambda p: values[p] if p in values else tile(ref, 8 * p)


def end_sweeps(get, refs, first, coefs_of, g_of):
    for n, ref in enumerate(refs):
        values = {}
        for p in sum(ends(first + n), []):
            here, near = around(get, p)
            values[p] = renewed(here, g_of(p), coefs_of(p), near)
        get = known(values, ref)
    return get, values


def end_layers(get, layers, coefs_of, g_of, weight_of):
    sums = []
    for planes in ends(8):
        parts = []
        for p in planes:
            here, near = around(get, p)
            parts.append(remaining(here, g_of(p), weight_of(p), coefs_of(p), near))
        sums.append(sum(parts[1:], parts[0]))
    put(layers, 0, sums[0])
    put(layers, 120, sums[1])


def ends_kernel(
    own, z_lo, z_hi, u1, u2, u3, inner, clayers, *rest
):
    held, (new, send, layers) = rest[:9], (rest[9:18], rest[18], rest[19])
    gz = lax.axis_index("gz")
    inside = place(iota(0))
    low, high = inside & (gz > 0), inside & (gz < NGZ - 1)
    cond, rhs = finish(own.at[1], z_lo.at[1], z_hi.at[1]), finish(own.at[0], z_lo.at[0], z_hi.at[0])
    table = {}
    for p in sum(ends(1), []):
        mask = low if p < HALO else high if p >= PLANES - HALO else inside
        c, near = around(cond, p)
        table[p] = coefs_at(mask, c, near, rhs(p))
        for ref, value in zip(new, (*table[p][0], *table[p][1:])):
            put(ref, 8 * p, value)

    def coefs_of(p):
        return table[p][0] if p in table else [tile(ref, 8 * p) for ref in held[:6]]

    def g_of(p):
        return table[p][1] if p in table else tile(held[6], 8 * p)

    def weight_of(p):
        return table[p][2] if p in table else tile(held[7], 8 * p)

    start = known({p: entry[1] for p, entry in table.items()}, u1)
    get, values = end_sweeps(start, (u2, u3, held[8]), 2, coefs_of, g_of)
    for p, value in values.items():
        put(new[8], 8 * p, value)
    for n in range(1, 15):
        put(layers, 8 * n, tile(inner, 8 * n))
    end_layers(get, layers, coefs_of, g_of, weight_of)
    scaled = [piece * (1.0 / 64.0) for piece in coarse_pieces(clayers)]
    send_rows(send, coarse_pieces(layers), scaled)


def ends_again_kernel(
    own, z_lo, z_hi, u1, u2, u3, inner, hxm, hxp, hym, hyp, hzm, hzp, source, weight, u4, new, send, layers
):
    def coefs_of(p):
        return [tile(ref, 8 * p) for ref in (hxm, hxp, hym, hyp, hzm, hzp)]

    def g_of(p):
        return tile(source, 8 * p)

    def weight_of(p):
        return tile(weight, 8 * p)

    start = finish(own.at[0], z_lo.at[0], z_hi.at[0])
    get, values = end_sweeps(start, (u1, u2, u3, u4), 1, coefs_of, g_of)
    for p, value in values.items():
        put(new, 8 * p, value)
    for n in range(1, 15):
        put(layers, 8 * n, tile(inner, 8 * n))
    end_layers(get, layers, coefs_of, g_of, weight_of)
    pieces = coarse_pieces(layers)
    send_rows(send, pieces, pieces)


KEYS = [(h, i, j, t) for h in range(2) for i in range(2) for j in range(2) for t in range(2)]


def coarse_tiles(half, table):
    out = {}
    for h, i, j, t in KEYS:
        row = half * 64 + i * 32 + j * 16 + t * 8
        out[h, i, j, t] = table[h][row : row + 8]
    return out


def coarse_neighbours(e):
    out = {}
    lane, sub = iota(1), iota(0)
    down = {key: subs(v, -1) for key, v in e.items()}
    up = {key: subs(v, 1) for key, v in e.items()}
    turned = {key: lanes(v, 32 if key[1] else -32) for key, v in e.items()}
    for h, i, j, t in KEYS:
        own, other = turned[h, 1 - i, j, t], turned[1 - h, 1 - i, j, t]
        if i == 0:
            xm, xp = jnp.where(lane >= 32, own, other), e[h, 1, j, t]
        else:
            xm, xp = e[h, 0, j, t], jnp.where(lane < 96, own, other)
        if j == 0:
            ym, yp = lanes(e[h, i, 1, t], 4), e[h, i, 1, t]
        else:
            ym, yp = e[h, i, 0, t], lanes(e[h, i, 0, t], -4)
        other_up, other_down = up[h, i, j, 1 - t], down[h, i, j, 1 - t]
        if t == 0:
            other_up = lanes(other_up, 1)
        else:
            other_down = lanes(other_down, -1)
        zm = jnp.where(sub > 0, up[h, i, j, t], other_up)
        zp = jnp.where(sub < 7, down[h, i, j, t], other_down)
        out[h, i, j, t] = (xm, xp, ym, yp, zm, zp)
    return out


def coarse_open(h, i, j, t):
    lane, sub = iota(1), iota(0)
    x = 2 * (4 * h + lane // 32) + i
    y = 2 * ((lane // 4) % 8) + j
    z = 16 * (lane % 4) + 8 * t + sub
    return x > 0, x < 2 * NGX - 1, y > 0, y < 2 * NGY - 1, z > 0, z < 16 * NGZ - 1


def coarse_solve(first, rhs, cc, cg, ext):
    table = [first[pl.ds(128 * h, 128), :].T for h in range(2)]
    cond = coarse_tiles(1, table)
    if rhs is not first:
        table = [rhs[pl.ds(128 * h, 128), :].T for h in range(2)]
    load = coarse_tiles(0, table)
    near = coarse_neighbours(cond)
    e = {}
    for n, key in enumerate(KEYS):
        open_sides = coarse_open(*key)
        faces = [cond[key] + jnp.where(o, v, 0.0) for o, v in zip(open_sides, near[key])]
        diag = ((faces[0] + faces[1]) + (faces[2] + faces[3])) + (faces[4] + faces[5])
        w = OMEGA / diag
        for m in range(6):
            cc[n, m] = jnp.where(open_sides[m], w * faces[m], 0.0)
        e[key] = (w + w) * load[key]
        cg[n] = e[key]

    def coarse_sweep(_, values):
        old = dict(zip(KEYS, values))
        near = coarse_neighbours(old)
        new = []
        for n, key in enumerate(KEYS):
            parts = [cc[n, m] * v for m, v in enumerate(near[key])]
            total = (parts[0] + parts[1]) + (parts[2] + parts[3])
            new.append((KEEP * old[key] + cg[n]) + total + (parts[4] + parts[5]))
        return new

    e = dict(zip(KEYS, lax.fori_loop(0, CSWEEPS - 1, coarse_sweep, [e[key] for key in KEYS])))
    sub = iota(0)
    for h, i, j, t in KEYS:
        if t == 0:
            low, high = subs(e[h, i, j, 0], 1), subs(e[h, i, j, 1], 1)
            at = 24 * (4 * h + 2 * i + j)
            ext[pl.ds(at, 8), :] = jnp.where(sub > 0, low, lanes(high, 1))
            ext[pl.ds(at + 8, 8), :] = jnp.where(sub > 0, high, low)
            ext[pl.ds(at + 16, 8), :] = jnp.where(sub == 0, high, lanes(low, -1))


def coarse_lines(ext):
    gx, gy, gz = (lax.axis_index(name) for name in AXES)
    shape = (24, 128)
    part = iota(1, shape) // 8
    x = 2 * gx - 1 + part // 4
    y = 2 * gy - 1 + part % 4
    z = 16 * gz - 1 + iota(0, shape)
    inside = (x >= 0) & (x < 2 * NGX) & (y >= 0) & (y < 2 * NGY) & (z >= 0) & (z < 16 * NGZ)
    sides = ((-1, 1), (0, 0), (0, 1), (1, 0))
    total = jnp.zeros(shape, F32)
    for n, (a, i) in enumerate(sides):
        px = (gx + a + NGX) % NGX
        for m, (b, j) in enumerate(sides):
            py = (gy + b + NGY) % NGY
            lane = (px % 4) * 32 + py * 4 + gz
            at = pl.multiple_of(24 * (4 * (px // 4) + 2 * i + j), 8)
            near = pltpu.roll(ext[pl.ds(at, 24), :], (128 - lane) % 128, 1)
            total = jnp.where(part == 4 * n + m, jnp.broadcast_to(near[:, :1], shape), total)
    return jnp.where(inside, total, 0.0)


def correct_kernel(
    split, first, rhs, u, hxm, hxp, hym, hyp, hzm, hzp, source, *rest
):
    outs, (buf, other, cc, cg, ext) = rest[: 1 + split], rest[1 + split :]
    coarse_solve(first, first if split else rhs, cc, cg, ext)
    lines = coarse_lines(ext)
    for t in range(PLANES // 8):
        layer = jnp.broadcast_to(lines[t : t + 1], (8, 128))
        for plane in range(max(8 * t, 4), min(8 * t + 8, PLANES - 4)):
            put(buf, 8 * plane, tile(u, 8 * plane) + layer)
    for plane in (3, PLANES - 4):
        put(buf, 8 * plane, jnp.zeros((8, 128), F32))
    coefs = (hxm, hxp, hym, hyp, hzm, hzp)
    sweep(buf, other, coefs, source, AFTER[0])
    sweep(other, buf, coefs, source, AFTER[1])
    sweep(buf, other, coefs, source, AFTER[2])
    sweep(other, buf, coefs, source, AFTER[3])
    for sub in range(8):
        block = buf[pl.ds(STEP + sub, BZ, stride=8), :].T
        for g in (1, 2):
            x = 8 * g - 8 + sub
            own = block[32 * g + 8 : 32 * g + 24]
            if split:
                outs[0][0, x] = own[:8]
                outs[1][0, x] = own[8:]
            else:
                outs[0][x] = own


def ring(value, axis, size, by):
    return lax.ppermute(value, axis, [(n, (n + by) % size) for n in range(size)])


def from_both(low, high, axis, size):
    return ring(high, axis, size, 1), ring(low, axis, size, -1)


def spread_planes(own_lo, own_hi):
    y_lo, y_hi = from_both(own_lo, own_hi, "gy", NGY)
    lows = [part[:, :8] for part in (y_lo, own_lo, own_hi, y_hi)]
    highs = [part[:, 8:] for part in (y_lo, own_lo, own_hi, y_hi)]
    x_lo, x_hi = from_both(
        jnp.concatenate(lows, axis=2), jnp.concatenate(highs, axis=2), "gx", NGX
    )
    own, z_lo, z_hi = turn(own_lo, own_hi, y_lo, y_hi, x_lo, x_hi)
    return (own, *from_both(z_lo, z_hi, "gz", NGZ))


def everywhere(send):
    return lax.all_to_all(send, AXES, 0, 0, tiled=True)


def correct(split, first, rhs, u, coefs, source):
    return call(
        functools.partial(correct_kernel, split),
        [(1, BX, 8, 128)] * 2 if split else [(BX, BY, BZ)],
        [(ROWS, 128), (ROWS, 128), (16, 6, 8, 128), (16, 8, 128), (8 * 24, 128)],
        first, rhs, u, *coefs, source,
    )


def body(right_side, conductivity):
    both = jnp.stack([right_side, conductivity])
    own, z_lo, z_hi = spread_planes(both[:, :, :8], both[:, :, 8:])
    *held, u1, u2, u3, u4, layers, clayers = call(
        inner_kernel, [(ROWS, 128)] * 12 + [(128, 128)] * 2, [], own, cost=COST
    )
    *coefs, source, weight, u, send = call(
        ends_kernel,
        [(ROWS, 128)] * 9 + [(DEVICES, 128)],
        [(128, 128)],
        own, z_lo, z_hi, u1, u2, u3, layers, clayers, *held, u4,
        aliases={8 + n: n for n in range(9)},
    )
    first = everywhere(send)
    halves = correct(True, first, first, u, coefs, source)
    own, z_lo, z_hi = spread_planes(*halves)
    u1, u2, u3, u4, layers = call(
        inner_again_kernel,
        [(ROWS, 128)] * 4 + [(128, 128)],
        [],
        own, *coefs, source, weight, cost=COST,
    )
    u, send = call(
        ends_again_kernel,
        [(ROWS, 128), (DEVICES, 128)],
        [(128, 128)],
        own, z_lo, z_hi, u1, u2, u3, layers, *coefs, source, weight, u4,
        aliases={15: 0},
    )
    return correct(False, first, everywhere(send), u, coefs, source)[0]


def solution(mesh):
    return jax.shard_map(
        body,
        mesh=mesh,
        in_specs=(P("gx", "gy", "gz"), P("gx", "gy", "gz")),
        out_specs=P("gx", "gy", "gz"),
        check_vma=False,
    )
```

```python
import functools

import jax
import jax.numpy as jnp
from jax import lax
from jax.experimental import pallas as pl
from jax.experimental.pallas import tpu as pltpu
from jax.sharding import PartitionSpec as P

SWEEPS = 4
CSWEEPS = 8
OMEGA = 0.8
KEEP = 0.2
AXES = ("gx", "gy", "gz")
NGX, NGY, NGZ = 8, 8, 4
BX, BY, BZ = 16, 16, 128
HALO = 8
PLANES = BZ + 2 * HALO
STEP = HALO * 8
ROWS = PLANES * 8
DEVICES = NGX * NGY * NGZ
F32 = jnp.float32
VMEM_LIMIT = 24 * 1024 * 1024
COST = 8_000_000
AFTER = ((4, 136, 1), (6, 132, 1), (7, 130, 1), (8, 128, 1))
INNER = ((9, 126, 3), (10, 124, 4), (11, 122, 2), (12, 120, 3))


def call(kernel, outs, scratch, *args, aliases={}, cost=None):
    if cost is not None:
        cost = pl.CostEstimate(flops=cost, bytes_accessed=cost, transcendentals=0)
    return pl.pallas_call(
        kernel,
        out_shape=[jax.ShapeDtypeStruct(shape, F32) for shape in outs],
        in_specs=[pl.BlockSpec(memory_space=pltpu.VMEM)] * len(args),
        out_specs=[pl.BlockSpec(memory_space=pltpu.VMEM)] * len(outs),
        scratch_shapes=[pltpu.VMEM(shape, F32) for shape in scratch],
        input_output_aliases=aliases,
        cost_estimate=cost,
        compiler_params=pltpu.CompilerParams(vmem_limit_bytes=VMEM_LIMIT),
    )(*args)


def iota(dim, shape=(8, 128)):
    return lax.broadcasted_iota(jnp.int32, shape, dim)


def lanes(v, by):
    return pltpu.roll(v, by % 128, 1)


def subs(v, by):
    return pltpu.roll(v, by % 8, 0)


def east(v):
    turned = subs(v, -1)
    return jnp.where(iota(0) < 7, turned, lanes(turned, -32))


def west(v):
    turned = subs(v, 1)
    return jnp.where(iota(0) > 0, turned, lanes(turned, 32))


def tile(ref, row):
    return ref[pl.ds(pl.multiple_of(row, 8), 8), :]


def put(ref, row, value):
    ref[pl.ds(pl.multiple_of(row, 8), 8), :] = value


def turns(start, count, times, step):
    per = count // times
    rims = iota(0) > 0, iota(0) < 7

    def body(n, _):
        step(pl.multiple_of((start + n * per) * 8, 8), per, rims)
        return 0

    lax.fori_loop(0, times, body, 0)


def place(sub):
    gx, gy = (lax.axis_index(name) for name in AXES[:2])
    lane = iota(1, sub.shape)
    x = gx * BX - HALO + 8 * (lane // 32) + sub
    y = gy * BY - HALO + lane % 32
    return (x >= 0) & (x < NGX * BX) & (y >= 0) & (y < NGY * BY)


def turn_kernel(count, own_lo, own_hi, y_lo, y_hi, x_lo, x_hi, out, z_lo, z_hi):
    for sub in range(8):
        inside = place(jnp.full((8, 128), sub, jnp.int32))
        for a in range(count):
            pieces = [x_lo[a, sub]]
            for x in (sub, 8 + sub):
                pieces += [y_lo[a, x], own_lo[a, x], own_hi[a, x], y_hi[a, x]]
            pieces += [x_hi[a, sub]]
            turned = jnp.concatenate(pieces, axis=0).T.reshape(BZ // 8, 8, 128)
            turned = jnp.where(inside[None], turned, 0.0).reshape(BZ, 128)
            out[a, pl.ds(STEP + sub, BZ, stride=8), :] = turned
            z_lo[a, pl.ds(sub, HALO, stride=8), :] = turned[:HALO]
            z_hi[a, pl.ds(sub, HALO, stride=8), :] = turned[BZ - HALO :]


def turn(own_lo, own_hi, y_lo, y_hi, x_lo, x_hi):
    count = own_lo.shape[0]
    return call(
        functools.partial(turn_kernel, count),
        [(count, ROWS, 128), (count, STEP, 128), (count, STEP, 128)],
        [],
        own_lo, own_hi, y_lo, y_hi, x_lo, x_hi,
    )


def walk(src, first, per, rims, visit):
    not_first, not_last = rims
    before, here = tile(src, first - 8), tile(src, first)
    base = None
    for n in range(per):
        if base is None or n >= base + 8:
            base = min(n, per - 8)
            start = pl.multiple_of(first + 8 * base, 8)
            ahead = lanes(src[pl.ds(start, 8, stride=8), :], -32)
            behind = lanes(src[pl.ds(start + 7, 8, stride=8), :], 32)
        after = tile(src, first + 8 * n + 8)
        xp = jnp.where(not_last, subs(here, -1), subs(ahead, 7 - (n - base)))
        xm = jnp.where(not_first, subs(here, 1), subs(behind, -(n - base)))
        visit(n, first + 8 * n, here, (xm, xp, lanes(here, 1), lanes(here, -1), before, after))
        before, here = here, after


def weighted(coefs, near):
    parts = [c * v for c, v in zip(coefs, near)]
    return ((parts[4] + parts[5]) + (parts[0] + parts[1])) + (parts[2] + parts[3])


def renewed(here, g, coefs, near):
    return (KEEP * here + g) + weighted(coefs, near)


def remaining(here, g, weight, coefs, near):
    return ((g - OMEGA * here) + weighted(coefs, near)) * weight


def sweep(src, dst, coefs, source, plan):
    def step(first, per, rims):
        def visit(n, row, here, near):
            put(dst, row, renewed(here, tile(source, row), [tile(ref, row) for ref in coefs], near))

        walk(src, first, per, rims, visit)

    turns(*plan, step)


def residual_layers(src, coefs, source, weight, layers):
    def step(first, per, rims):
        sums = [None]

        def visit(n, row, here, near):
            rest = remaining(
                here, tile(source, row), tile(weight, row), [tile(ref, row) for ref in coefs], near
            )
            sums[0] = rest if n % 8 == 0 else sums[0] + rest
            if n % 8 == 7:
                put(layers, (first - STEP) // 8 + n - 7, sums[0])

        walk(src, first, per, rims, visit)

    turns(16, 112, 2, step)


def coarse_pieces(layers):
    lane = iota(1, (16, 128))
    rows = [layers[pl.ds(sub, 16, stride=8), :] for sub in range(8)]
    row = ((rows[0] + rows[1]) + (rows[2] + rows[3])) + ((rows[4] + rows[5]) + (rows[6] + rows[7]))
    return [jnp.where(lane // 8 == 5 + 4 * i + j, row, 0.0) for i in range(2) for j in range(2)]


def send_rows(send, left, right):
    table = jnp.concatenate(left + right, axis=0)
    turned = table.T.reshape(16, 8, 128)
    line = jnp.broadcast_to(turned.sum(axis=0).sum(axis=0, keepdims=True), (8, 128))
    send[...] = jnp.concatenate([line] * (DEVICES // 8), axis=0)


def coefs_at(inside, c, near, rhs):
    faces = [c + v for v in near]
    diag = ((faces[0] + faces[1]) + (faces[2] + faces[3])) + (faces[4] + faces[5])
    w = jnp.where(inside, OMEGA / jnp.where(inside, diag, 1.0), 0.0)
    return [w * face for face in faces], (w + w) * rhs, diag * (0.5 / OMEGA)


def inner_kernel(
    own, hxm, hxp, hym, hyp, hzm, hzp, source, weight, u1, u2, u3, u4, layers, clayers
):
    coefs = (hxm, hxp, hym, hyp, hzm, hzp)
    inside = place(iota(0))

    def coefs_of(first, per, rims):
        def visit(n, row, c, near):
            held, g, rest = coefs_at(inside, c, near, tile(own.at[0], row))
            for ref, value in zip(coefs, held):
                put(ref, row, value)
            put(source, row, g)
            put(weight, row, rest)
            put(u1, row, g)

        walk(own.at[1], first, per, rims, visit)

    turns(*INNER[0], coefs_of)
    for n in range(16):
        put(clayers, 8 * n, sum(tile(own.at[1], STEP + STEP * n + 8 * m) for m in range(8)))
    sweep(u1, u2, coefs, source, INNER[1])
    sweep(u2, u3, coefs, source, INNER[2])
    sweep(u3, u4, coefs, source, INNER[3])
    residual_layers(u4, coefs, source, weight, layers)


def inner_again_kernel(
    own, hxm, hxp, hym, hyp, hzm, hzp, source, weight, u1, u2, u3, u4, layers
):
    coefs = (hxm, hxp, hym, hyp, hzm, hzp)
    sweep(own.at[0], u1, coefs, source, INNER[0])
    sweep(u1, u2, coefs, source, INNER[1])
    sweep(u2, u3, coefs, source, INNER[2])
    sweep(u3, u4, coefs, source, INNER[3])
    residual_layers(u4, coefs, source, weight, layers)


def ends(first, count=8):
    return list(range(first, first + count)), list(range(PLANES - first - count, PLANES - first))


def around(get, p):
    here = get(p)
    return here, (west(here), east(here), lanes(here, 1), lanes(here, -1), get(p - 1), get(p + 1))


def finish(own, z_lo, z_hi):
    gz = lax.axis_index("gz")

    def get(p):
        if p < HALO:
            return jnp.where(gz > 0, tile(z_lo, 8 * p), 0.0)
        if p >= PLANES - HALO:
            return jnp.where(gz < NGZ - 1, tile(z_hi, 8 * (p - PLANES + HALO)), 0.0)
        return tile(own, 8 * p)

    return get


def known(values, ref):
    return lambda p: values[p] if p in values else tile(ref, 8 * p)


def end_sweeps(get, refs, first, coefs_of, g_of):
    for n, ref in enumerate(refs):
        values = {}
        for p in sum(ends(first + n), []):
            here, near = around(get, p)
            values[p] = renewed(here, g_of(p), coefs_of(p), near)
        get = known(values, ref)
    return get, values


def end_layers(get, layers, coefs_of, g_of, weight_of):
    sums = []
    for planes in ends(8):
        parts = []
        for p in planes:
            here, near = around(get, p)
            parts.append(remaining(here, g_of(p), weight_of(p), coefs_of(p), near))
        sums.append(sum(parts[1:], parts[0]))
    put(layers, 0, sums[0])
    put(layers, 120, sums[1])


def ends_kernel(
    own, z_lo, z_hi, u1, u2, u3, inner, clayers, *rest
):
    held, (new, send, layers) = rest[:9], (rest[9:18], rest[18], rest[19])
    gz = lax.axis_index("gz")
    inside = place(iota(0))
    low, high = inside & (gz > 0), inside & (gz < NGZ - 1)
    cond, rhs = finish(own.at[1], z_lo.at[1], z_hi.at[1]), finish(own.at[0], z_lo.at[0], z_hi.at[0])
    table = {}
    for p in sum(ends(1), []):
        mask = low if p < HALO else high if p >= PLANES - HALO else inside
        c, near = around(cond, p)
        table[p] = coefs_at(mask, c, near, rhs(p))
        for ref, value in zip(new, (*table[p][0], *table[p][1:])):
            put(ref, 8 * p, value)

    def coefs_of(p):
        return table[p][0] if p in table else [tile(ref, 8 * p) for ref in held[:6]]

    def g_of(p):
        return table[p][1] if p in table else tile(held[6], 8 * p)

    def weight_of(p):
        return table[p][2] if p in table else tile(held[7], 8 * p)

    start = known({p: entry[1] for p, entry in table.items()}, u1)
    get, values = end_sweeps(start, (u2, u3, held[8]), 2, coefs_of, g_of)
    for p, value in values.items():
        put(new[8], 8 * p, value)
    for n in range(1, 15):
        put(layers, 8 * n, tile(inner, 8 * n))
    end_layers(get, layers, coefs_of, g_of, weight_of)
    scaled = [piece * (1.0 / 64.0) for piece in coarse_pieces(clayers)]
    send_rows(send, coarse_pieces(layers), scaled)


def ends_again_kernel(
    own, z_lo, z_hi, u1, u2, u3, inner, hxm, hxp, hym, hyp, hzm, hzp, source, weight, u4, new, send, layers
):
    def coefs_of(p):
        return [tile(ref, 8 * p) for ref in (hxm, hxp, hym, hyp, hzm, hzp)]

    def g_of(p):
        return tile(source, 8 * p)

    def weight_of(p):
        return tile(weight, 8 * p)

    start = finish(own.at[0], z_lo.at[0], z_hi.at[0])
    get, values = end_sweeps(start, (u1, u2, u3, u4), 1, coefs_of, g_of)
    for p, value in values.items():
        put(new, 8 * p, value)
    for n in range(1, 15):
        put(layers, 8 * n, tile(inner, 8 * n))
    end_layers(get, layers, coefs_of, g_of, weight_of)
    pieces = coarse_pieces(layers)
    send_rows(send, pieces, pieces)


KEYS = [(h, i, j, t) for h in range(2) for i in range(2) for j in range(2) for t in range(2)]


def coarse_tiles(half, table):
    out = {}
    for h, i, j, t in KEYS:
        row = half * 64 + i * 32 + j * 16 + t * 8
        out[h, i, j, t] = table[h][row : row + 8]
    return out


def coarse_neighbours(e):
    out = {}
    lane, sub = iota(1), iota(0)
    down = {key: subs(v, -1) for key, v in e.items()}
    up = {key: subs(v, 1) for key, v in e.items()}
    turned = {key: lanes(v, 32 if key[1] else -32) for key, v in e.items()}
    for h, i, j, t in KEYS:
        own, other = turned[h, 1 - i, j, t], turned[1 - h, 1 - i, j, t]
        if i == 0:
            xm, xp = jnp.where(lane >= 32, own, other), e[h, 1, j, t]
        else:
            xm, xp = e[h, 0, j, t], jnp.where(lane < 96, own, other)
        if j == 0:
            ym, yp = lanes(e[h, i, 1, t], 4), e[h, i, 1, t]
        else:
            ym, yp = e[h, i, 0, t], lanes(e[h, i, 0, t], -4)
        other_up, other_down = up[h, i, j, 1 - t], down[h, i, j, 1 - t]
        if t == 0:
            other_up = lanes(other_up, 1)
        else:
            other_down = lanes(other_down, -1)
        zm = jnp.where(sub > 0, up[h, i, j, t], other_up)
        zp = jnp.where(sub < 7, down[h, i, j, t], other_down)
        out[h, i, j, t] = (xm, xp, ym, yp, zm, zp)
    return out


def coarse_open(h, i, j, t):
    lane, sub = iota(1), iota(0)
    x = 2 * (4 * h + lane // 32) + i
    y = 2 * ((lane // 4) % 8) + j
    z = 16 * (lane % 4) + 8 * t + sub
    return x > 0, x < 2 * NGX - 1, y > 0, y < 2 * NGY - 1, z > 0, z < 16 * NGZ - 1


def coarse_coefs(table, cc, cw):
    cond = coarse_tiles(1, table)
    near = coarse_neighbours(cond)
    for n, key in enumerate(KEYS):
        open_sides = coarse_open(*key)
        faces = [cond[key] + jnp.where(o, v, 0.0) for o, v in zip(open_sides, near[key])]
        diag = ((faces[0] + faces[1]) + (faces[2] + faces[3])) + (faces[4] + faces[5])
        w = OMEGA / diag
        for m in range(6):
            cc[n, m] = jnp.where(open_sides[m], w * faces[m], 0.0)
        cw[n] = w + w


def coarse_solve(table, cc, cw, cg, ext):
    load = coarse_tiles(0, table)
    e = {}
    for n, key in enumerate(KEYS):
        e[key] = cw[n] * load[key]
        cg[n] = e[key]

    def coarse_sweep(_, values):
        old = dict(zip(KEYS, values))
        near = coarse_neighbours(old)
        new = []
        for n, key in enumerate(KEYS):
            parts = [cc[n, m] * v for m, v in enumerate(near[key])]
            total = (parts[0] + parts[1]) + (parts[2] + parts[3])
            new.append((KEEP * old[key] + cg[n]) + total + (parts[4] + parts[5]))
        return new

    e = dict(zip(KEYS, lax.fori_loop(0, CSWEEPS - 1, coarse_sweep, [e[key] for key in KEYS])))
    sub = iota(0)
    for h, i, j, t in KEYS:
        if t == 0:
            low, high = subs(e[h, i, j, 0], 1), subs(e[h, i, j, 1], 1)
            at = 24 * (4 * h + 2 * i + j)
            ext[pl.ds(at, 8), :] = jnp.where(sub > 0, low, lanes(high, 1))
            ext[pl.ds(at + 8, 8), :] = jnp.where(sub > 0, high, low)
            ext[pl.ds(at + 16, 8), :] = jnp.where(sub == 0, high, lanes(low, -1))


def coarse_lines(ext):
    gx, gy, gz = (lax.axis_index(name) for name in AXES)
    shape = (24, 128)
    part = iota(1, shape) // 8
    x = 2 * gx - 1 + part // 4
    y = 2 * gy - 1 + part % 4
    z = 16 * gz - 1 + iota(0, shape)
    inside = (x >= 0) & (x < 2 * NGX) & (y >= 0) & (y < 2 * NGY) & (z >= 0) & (z < 16 * NGZ)
    lane = ((x // 2) % 4) * 32 + ((y // 2) % 8) * 4 + gz
    group = 4 * ((x // 8) % 2) + 2 * (x % 2) + y % 2
    total = jnp.zeros(shape, F32)
    for n in range(8):
        near = jnp.take_along_axis(ext[pl.ds(24 * n, 24), :], lane, axis=1)
        total = jnp.where(group == n, near, total)
    return jnp.where(inside, total, 0.0)


def correct_kernel(split, rhs, u, hxm, hxp, hym, hyp, hzm, hzp, source, *rest):
    table = [rhs[pl.ds(128 * h, 128), :].T for h in range(2)]
    if split:
        *outs, cc, cw, buf, other, cg, ext = rest
        coarse_coefs(table, cc, cw)
    else:
        cc, cw, *outs, buf, other, cg, ext = rest
    coarse_solve(table, cc, cw, cg, ext)
    lines = coarse_lines(ext)
    for t in range(PLANES // 8):
        layer = jnp.broadcast_to(lines[t : t + 1], (8, 128))
        for plane in range(max(8 * t, 4), min(8 * t + 8, PLANES - 4)):
            put(buf, 8 * plane, tile(u, 8 * plane) + layer)
    for plane in (3, PLANES - 4):
        put(buf, 8 * plane, jnp.zeros((8, 128), F32))
    coefs = (hxm, hxp, hym, hyp, hzm, hzp)
    sweep(buf, other, coefs, source, AFTER[0])
    sweep(other, buf, coefs, source, AFTER[1])
    sweep(buf, other, coefs, source, AFTER[2])
    sweep(other, buf, coefs, source, AFTER[3])
    for sub in range(8):
        block = buf[pl.ds(STEP + sub, BZ, stride=8), :].T
        for g in (1, 2):
            x = 8 * g - 8 + sub
            own = block[32 * g + 8 : 32 * g + 24]
            if split:
                outs[0][0, x] = own[:8]
                outs[1][0, x] = own[8:]
            else:
                outs[0][x] = own


def ring(value, axis, size, by):
    return lax.ppermute(value, axis, [(n, (n + by) % size) for n in range(size)])


def from_both(low, high, axis, size):
    return ring(high, axis, size, 1), ring(low, axis, size, -1)


def spread_planes(own_lo, own_hi):
    y_lo, y_hi = from_both(own_lo, own_hi, "gy", NGY)
    lows = [part[:, :8] for part in (y_lo, own_lo, own_hi, y_hi)]
    highs = [part[:, 8:] for part in (y_lo, own_lo, own_hi, y_hi)]
    x_lo, x_hi = from_both(
        jnp.concatenate(lows, axis=2), jnp.concatenate(highs, axis=2), "gx", NGX
    )
    own, z_lo, z_hi = turn(own_lo, own_hi, y_lo, y_hi, x_lo, x_hi)
    return (own, *from_both(z_lo, z_hi, "gz", NGZ))


def everywhere(send):
    return lax.all_to_all(send, AXES, 0, 0, tiled=True)


def correct(rhs, u, coefs, source, *kept):
    outs = [(BX, BY, BZ)] if kept else [(1, BX, 8, 128)] * 2 + [(16, 6, 8, 128), (16, 8, 128)]
    return call(
        functools.partial(correct_kernel, not kept),
        outs,
        [(ROWS, 128), (ROWS, 128), (16, 8, 128), (8 * 24, 128)],
        rhs, u, *coefs, source, *kept,
    )


def body(right_side, conductivity):
    both = jnp.stack([right_side, conductivity])
    own, z_lo, z_hi = spread_planes(both[:, :, :8], both[:, :, 8:])
    *held, u1, u2, u3, u4, layers, clayers = call(
        inner_kernel, [(ROWS, 128)] * 12 + [(128, 128)] * 2, [], own, cost=COST
    )
    *coefs, source, weight, u, send = call(
        ends_kernel,
        [(ROWS, 128)] * 9 + [(DEVICES, 128)],
        [(128, 128)],
        own, z_lo, z_hi, u1, u2, u3, layers, clayers, *held, u4,
        aliases={8 + n: n for n in range(9)},
    )
    own_lo, own_hi, *kept = correct(everywhere(send), u, coefs, source)
    own, z_lo, z_hi = spread_planes(own_lo, own_hi)
    u1, u2, u3, u4, layers = call(
        inner_again_kernel,
        [(ROWS, 128)] * 4 + [(128, 128)],
        [],
        own, *coefs, source, weight, cost=COST,
    )
    u, send = call(
        ends_again_kernel,
        [(ROWS, 128), (DEVICES, 128)],
        [(128, 128)],
        own, z_lo, z_hi, u1, u2, u3, layers, *coefs, source, weight, u4,
        aliases={15: 0},
    )
    return correct(everywhere(send), u, coefs, source, *kept)[0]


def solution(mesh):
    return jax.shard_map(
        body,
        mesh=mesh,
        in_specs=(P("gx", "gy", "gz"), P("gx", "gy", "gz")),
        out_specs=P("gx", "gy", "gz"),
        check_vma=False,
    )
```

```python
import functools

import jax
import jax.numpy as jnp
from jax import lax
from jax.experimental import pallas as pl
from jax.experimental.pallas import tpu as pltpu
from jax.sharding import PartitionSpec as P

SWEEPS = 4
CSWEEPS = 8
OMEGA = 0.8
KEEP = 0.2
AXES = ("gx", "gy", "gz")
NGX, NGY, NGZ = 8, 8, 4
BX, BY, BZ = 16, 16, 128
HALO = 8
PLANES = BZ + 2 * HALO
STEP = HALO * 8
ROWS = PLANES * 8
DEVICES = NGX * NGY * NGZ
F32 = jnp.float32
VMEM_LIMIT = 24 * 1024 * 1024
COST = 8_000_000
AFTER = ((4, 136, 1), (6, 132, 1), (7, 130, 1), (8, 128, 1))
INNER = ((9, 126, 2), (10, 124, 2), (11, 122, 1), (12, 120, 1))


def call(kernel, outs, scratch, *args, aliases={}, cost=None):
    if cost is not None:
        cost = pl.CostEstimate(flops=cost, bytes_accessed=cost, transcendentals=0)
    return pl.pallas_call(
        kernel,
        out_shape=[jax.ShapeDtypeStruct(shape, F32) for shape in outs],
        in_specs=[pl.BlockSpec(memory_space=pltpu.VMEM)] * len(args),
        out_specs=[pl.BlockSpec(memory_space=pltpu.VMEM)] * len(outs),
        scratch_shapes=[pltpu.VMEM(shape, F32) for shape in scratch],
        input_output_aliases=aliases,
        cost_estimate=cost,
        compiler_params=pltpu.CompilerParams(vmem_limit_bytes=VMEM_LIMIT),
    )(*args)


def iota(dim, shape=(8, 128)):
    return lax.broadcasted_iota(jnp.int32, shape, dim)


def lanes(v, by):
    return pltpu.roll(v, by % 128, 1)


def subs(v, by):
    return pltpu.roll(v, by % 8, 0)


def east(v):
    turned = subs(v, -1)
    return jnp.where(iota(0) < 7, turned, lanes(turned, -32))


def west(v):
    turned = subs(v, 1)
    return jnp.where(iota(0) > 0, turned, lanes(turned, 32))


def tile(ref, row):
    return ref[pl.ds(pl.multiple_of(row, 8), 8), :]


def put(ref, row, value):
    ref[pl.ds(pl.multiple_of(row, 8), 8), :] = value


def turns(start, count, times, step):
    per = count // times
    rims = iota(0) > 0, iota(0) < 7

    def body(n, _):
        step(pl.multiple_of((start + n * per) * 8, 8), per, rims)
        return 0

    lax.fori_loop(0, times, body, 0)


def place(sub):
    gx, gy = (lax.axis_index(name) for name in AXES[:2])
    lane = iota(1, sub.shape)
    x = gx * BX - HALO + 8 * (lane // 32) + sub
    y = gy * BY - HALO + lane % 32
    return (x >= 0) & (x < NGX * BX) & (y >= 0) & (y < NGY * BY)


def turn_kernel(count, own_lo, own_hi, y_lo, y_hi, x_lo, x_hi, out, z_lo, z_hi):
    for sub in range(8):
        inside = place(jnp.full((8, 128), sub, jnp.int32))
        for a in range(count):
            pieces = [x_lo[a, sub]]
            for x in (sub, 8 + sub):
                pieces += [y_lo[a, x], own_lo[a, x], own_hi[a, x], y_hi[a, x]]
            pieces += [x_hi[a, sub]]
            turned = jnp.concatenate(pieces, axis=0).T.reshape(BZ // 8, 8, 128)
            turned = jnp.where(inside[None], turned, 0.0).reshape(BZ, 128)
            out[a, pl.ds(STEP + sub, BZ, stride=8), :] = turned
            z_lo[a, pl.ds(sub, HALO, stride=8), :] = turned[:HALO]
            z_hi[a, pl.ds(sub, HALO, stride=8), :] = turned[BZ - HALO :]


def turn(own_lo, own_hi, y_lo, y_hi, x_lo, x_hi):
    count = own_lo.shape[0]
    return call(
        functools.partial(turn_kernel, count),
        [(count, ROWS, 128), (count, STEP, 128), (count, STEP, 128)],
        [],
        own_lo, own_hi, y_lo, y_hi, x_lo, x_hi,
    )


def walk(src, first, per, rims, visit):
    not_first, not_last = rims
    before, here = tile(src, first - 8), tile(src, first)
    base = None
    for n in range(per):
        if base is None or n >= base + 8:
            base = min(n, per - 8)
            start = pl.multiple_of(first + 8 * base, 8)
            ahead = lanes(src[pl.ds(start, 8, stride=8), :], -32)
            behind = lanes(src[pl.ds(start + 7, 8, stride=8), :], 32)
        after = tile(src, first + 8 * n + 8)
        xp = jnp.where(not_last, subs(here, -1), subs(ahead, 7 - (n - base)))
        xm = jnp.where(not_first, subs(here, 1), subs(behind, -(n - base)))
        visit(n, first + 8 * n, here, (xm, xp, lanes(here, 1), lanes(here, -1), before, after))
        before, here = here, after


def weighted(coefs, near):
    parts = [c * v for c, v in zip(coefs, near)]
    return ((parts[4] + parts[5]) + (parts[0] + parts[1])) + (parts[2] + parts[3])


def renewed(here, g, coefs, near):
    return (KEEP * here + g) + weighted(coefs, near)


def remaining(here, g, weight, coefs, near):
    return ((g - OMEGA * here) + weighted(coefs, near)) * weight


def sweep(src, dst, coefs, source, plan):
    def step(first, per, rims):
        def visit(n, row, here, near):
            put(dst, row, renewed(here, tile(source, row), [tile(ref, row) for ref in coefs], near))

        walk(src, first, per, rims, visit)

    turns(*plan, step)


def residual_layers(src, coefs, source, weight, layers):
    def step(first, per, rims):
        sums = [None]

        def visit(n, row, here, near):
            rest = remaining(
                here, tile(source, row), tile(weight, row), [tile(ref, row) for ref in coefs], near
            )
            sums[0] = rest if n % 8 == 0 else sums[0] + rest
            if n % 8 == 7:
                put(layers, (first - STEP) // 8 + n - 7, sums[0])

        walk(src, first, per, rims, visit)

    turns(16, 112, 2, step)


def coarse_pieces(layers):
    lane = iota(1, (16, 128))
    rows = [layers[pl.ds(sub, 16, stride=8), :] for sub in range(8)]
    row = ((rows[0] + rows[1]) + (rows[2] + rows[3])) + ((rows[4] + rows[5]) + (rows[6] + rows[7]))
    return [jnp.where(lane // 8 == 5 + 4 * i + j, row, 0.0) for i in range(2) for j in range(2)]


def send_rows(send, left, right):
    table = jnp.concatenate(left + right, axis=0)
    turned = table.T.reshape(16, 8, 128)
    line = jnp.broadcast_to(turned.sum(axis=0).sum(axis=0, keepdims=True), (8, 128))
    send[...] = jnp.concatenate([line] * (DEVICES // 8), axis=0)


def coefs_at(inside, c, near, rhs):
    faces = [c + v for v in near]
    diag = ((faces[0] + faces[1]) + (faces[2] + faces[3])) + (faces[4] + faces[5])
    w = jnp.where(inside, OMEGA / jnp.where(inside, diag, 1.0), 0.0)
    return [w * face for face in faces], (w + w) * rhs, diag * (0.5 / OMEGA)


def inner_kernel(
    own, hxm, hxp, hym, hyp, hzm, hzp, source, weight, u1, u2, u3, u4, layers, clayers
):
    coefs = (hxm, hxp, hym, hyp, hzm, hzp)
    inside = place(iota(0))

    def coefs_of(first, per, rims):
        def visit(n, row, c, near):
            held, g, rest = coefs_at(inside, c, near, tile(own.at[0], row))
            for ref, value in zip(coefs, held):
                put(ref, row, value)
            put(source, row, g)
            put(weight, row, rest)
            put(u1, row, g)

        walk(own.at[1], first, per, rims, visit)

    turns(*INNER[0], coefs_of)
    for n in range(16):
        put(clayers, 8 * n, sum(tile(own.at[1], STEP + STEP * n + 8 * m) for m in range(8)))
    sweep(u1, u2, coefs, source, INNER[1])
    sweep(u2, u3, coefs, source, INNER[2])
    sweep(u3, u4, coefs, source, INNER[3])
    residual_layers(u4, coefs, source, weight, layers)


def inner_again_kernel(
    own, hxm, hxp, hym, hyp, hzm, hzp, source, weight, u1, u2, u3, u4, layers
):
    coefs = (hxm, hxp, hym, hyp, hzm, hzp)
    sweep(own.at[0], u1, coefs, source, INNER[0])
    sweep(u1, u2, coefs, source, INNER[1])
    sweep(u2, u3, coefs, source, INNER[2])
    sweep(u3, u4, coefs, source, INNER[3])
    residual_layers(u4, coefs, source, weight, layers)


def ends(first, count=8):
    return list(range(first, first + count)), list(range(PLANES - first - count, PLANES - first))


def around(get, p):
    here = get(p)
    return here, (west(here), east(here), lanes(here, 1), lanes(here, -1), get(p - 1), get(p + 1))


def finish(own, z_lo, z_hi):
    gz = lax.axis_index("gz")

    def get(p):
        if p < HALO:
            return jnp.where(gz > 0, tile(z_lo, 8 * p), 0.0)
        if p >= PLANES - HALO:
            return jnp.where(gz < NGZ - 1, tile(z_hi, 8 * (p - PLANES + HALO)), 0.0)
        return tile(own, 8 * p)

    return get


def known(values, ref):
    return lambda p: values[p] if p in values else tile(ref, 8 * p)


def end_sweeps(get, refs, first, coefs_of, g_of):
    for n, ref in enumerate(refs):
        values = {}
        for p in sum(ends(first + n), []):
            here, near = around(get, p)
            values[p] = renewed(here, g_of(p), coefs_of(p), near)
        get = known(values, ref)
    return get, values


def end_layers(get, layers, coefs_of, g_of, weight_of):
    sums = []
    for planes in ends(8):
        parts = []
        for p in planes:
            here, near = around(get, p)
            parts.append(remaining(here, g_of(p), weight_of(p), coefs_of(p), near))
        sums.append(sum(parts[1:], parts[0]))
    put(layers, 0, sums[0])
    put(layers, 120, sums[1])


def ends_kernel(
    own, z_lo, z_hi, u1, u2, u3, inner, clayers, *rest
):
    held, (new, send, layers) = rest[:9], (rest[9:18], rest[18], rest[19])
    gz = lax.axis_index("gz")
    inside = place(iota(0))
    low, high = inside & (gz > 0), inside & (gz < NGZ - 1)
    cond, rhs = finish(own.at[1], z_lo.at[1], z_hi.at[1]), finish(own.at[0], z_lo.at[0], z_hi.at[0])
    table = {}
    for p in sum(ends(1), []):
        mask = low if p < HALO else high if p >= PLANES - HALO else inside
        c, near = around(cond, p)
        table[p] = coefs_at(mask, c, near, rhs(p))
        for ref, value in zip(new, (*table[p][0], *table[p][1:])):
            put(ref, 8 * p, value)

    def coefs_of(p):
        return table[p][0] if p in table else [tile(ref, 8 * p) for ref in held[:6]]

    def g_of(p):
        return table[p][1] if p in table else tile(held[6], 8 * p)

    def weight_of(p):
        return table[p][2] if p in table else tile(held[7], 8 * p)

    start = known({p: entry[1] for p, entry in table.items()}, u1)
    get, values = end_sweeps(start, (u2, u3, held[8]), 2, coefs_of, g_of)
    for p, value in values.items():
        put(new[8], 8 * p, value)
    for n in range(1, 15):
        put(layers, 8 * n, tile(inner, 8 * n))
    end_layers(get, layers, coefs_of, g_of, weight_of)
    scaled = [piece * (1.0 / 64.0) for piece in coarse_pieces(clayers)]
    send_rows(send, coarse_pieces(layers), scaled)


def ends_again_kernel(
    own, z_lo, z_hi, u1, u2, u3, inner, hxm, hxp, hym, hyp, hzm, hzp, source, weight, u4, new, send, layers
):
    def coefs_of(p):
        return [tile(ref, 8 * p) for ref in (hxm, hxp, hym, hyp, hzm, hzp)]

    def g_of(p):
        return tile(source, 8 * p)

    def weight_of(p):
        return tile(weight, 8 * p)

    start = finish(own.at[0], z_lo.at[0], z_hi.at[0])
    get, values = end_sweeps(start, (u1, u2, u3, u4), 1, coefs_of, g_of)
    for p, value in values.items():
        put(new, 8 * p, value)
    for n in range(1, 15):
        put(layers, 8 * n, tile(inner, 8 * n))
    end_layers(get, layers, coefs_of, g_of, weight_of)
    pieces = coarse_pieces(layers)
    send_rows(send, pieces, pieces)


KEYS = [(h, i, j, t) for h in range(2) for i in range(2) for j in range(2) for t in range(2)]


def coarse_tiles(half, table):
    out = {}
    for h, i, j, t in KEYS:
        row = half * 64 + i * 32 + j * 16 + t * 8
        out[h, i, j, t] = table[h][row : row + 8]
    return out


def coarse_neighbours(e):
    out = {}
    lane, sub = iota(1), iota(0)
    down = {key: subs(v, -1) for key, v in e.items()}
    up = {key: subs(v, 1) for key, v in e.items()}
    turned = {key: lanes(v, 32 if key[1] else -32) for key, v in e.items()}
    for h, i, j, t in KEYS:
        own, other = turned[h, 1 - i, j, t], turned[1 - h, 1 - i, j, t]
        if i == 0:
            xm, xp = jnp.where(lane >= 32, own, other), e[h, 1, j, t]
        else:
            xm, xp = e[h, 0, j, t], jnp.where(lane < 96, own, other)
        if j == 0:
            ym, yp = lanes(e[h, i, 1, t], 4), e[h, i, 1, t]
        else:
            ym, yp = e[h, i, 0, t], lanes(e[h, i, 0, t], -4)
        other_up, other_down = up[h, i, j, 1 - t], down[h, i, j, 1 - t]
        if t == 0:
            other_up = lanes(other_up, 1)
        else:
            other_down = lanes(other_down, -1)
        zm = jnp.where(sub > 0, up[h, i, j, t], other_up)
        zp = jnp.where(sub < 7, down[h, i, j, t], other_down)
        out[h, i, j, t] = (xm, xp, ym, yp, zm, zp)
    return out


def coarse_open(h, i, j, t):
    lane, sub = iota(1), iota(0)
    x = 2 * (4 * h + lane // 32) + i
    y = 2 * ((lane // 4) % 8) + j
    z = 16 * (lane % 4) + 8 * t + sub
    return x > 0, x < 2 * NGX - 1, y > 0, y < 2 * NGY - 1, z > 0, z < 16 * NGZ - 1


def coarse_coefs(table, cc, cw):
    cond = coarse_tiles(1, table)
    near = coarse_neighbours(cond)
    for n, key in enumerate(KEYS):
        open_sides = coarse_open(*key)
        faces = [cond[key] + jnp.where(o, v, 0.0) for o, v in zip(open_sides, near[key])]
        diag = ((faces[0] + faces[1]) + (faces[2] + faces[3])) + (faces[4] + faces[5])
        w = OMEGA / diag
        for m in range(6):
            cc[n, m] = jnp.where(open_sides[m], w * faces[m], 0.0)
        cw[n] = w + w


def coarse_solve(table, cc, cw, cg, ext):
    load = coarse_tiles(0, table)
    e = {}
    for n, key in enumerate(KEYS):
        e[key] = cw[n] * load[key]
        cg[n] = e[key]

    def coarse_sweep(_, values):
        old = dict(zip(KEYS, values))
        near = coarse_neighbours(old)
        new = []
        for n, key in enumerate(KEYS):
            parts = [cc[n, m] * v for m, v in enumerate(near[key])]
            total = (parts[0] + parts[1]) + (parts[2] + parts[3])
            new.append((KEEP * old[key] + cg[n]) + total + (parts[4] + parts[5]))
        return new

    e = dict(zip(KEYS, lax.fori_loop(0, CSWEEPS - 1, coarse_sweep, [e[key] for key in KEYS])))
    sub = iota(0)
    for h, i, j, t in KEYS:
        if t == 0:
            low, high = subs(e[h, i, j, 0], 1), subs(e[h, i, j, 1], 1)
            at = 24 * (4 * h + 2 * i + j)
            ext[pl.ds(at, 8), :] = jnp.where(sub > 0, low, lanes(high, 1))
            ext[pl.ds(at + 8, 8), :] = jnp.where(sub > 0, high, low)
            ext[pl.ds(at + 16, 8), :] = jnp.where(sub == 0, high, lanes(low, -1))


def coarse_lines(ext):
    gx, gy, gz = (lax.axis_index(name) for name in AXES)
    shape = (24, 128)
    part = iota(1, shape) // 8
    x = 2 * gx - 1 + part // 4
    y = 2 * gy - 1 + part % 4
    z = 16 * gz - 1 + iota(0, shape)
    inside = (x >= 0) & (x < 2 * NGX) & (y >= 0) & (y < 2 * NGY) & (z >= 0) & (z < 16 * NGZ)
    lane = ((x // 2) % 4) * 32 + ((y // 2) % 8) * 4 + gz
    group = 4 * ((x // 8) % 2) + 2 * (x % 2) + y % 2
    total = jnp.zeros(shape, F32)
    for n in range(8):
        near = jnp.take_along_axis(ext[pl.ds(24 * n, 24), :], lane, axis=1)
        total = jnp.where(group == n, near, total)
    return jnp.where(inside, total, 0.0)


def correct_kernel(split, rhs, u, hxm, hxp, hym, hyp, hzm, hzp, source, *rest):
    table = [rhs[pl.ds(128 * h, 128), :].T for h in range(2)]
    if split:
        *outs, cc, cw, buf, other, cg, ext = rest
        coarse_coefs(table, cc, cw)
    else:
        cc, cw, *outs, buf, other, cg, ext = rest
    coarse_solve(table, cc, cw, cg, ext)
    lines = coarse_lines(ext)
    for t in range(PLANES // 8):
        layer = jnp.broadcast_to(lines[t : t + 1], (8, 128))
        for plane in range(max(8 * t, 4), min(8 * t + 8, PLANES - 4)):
            put(buf, 8 * plane, tile(u, 8 * plane) + layer)
    for plane in (3, PLANES - 4):
        put(buf, 8 * plane, jnp.zeros((8, 128), F32))
    coefs = (hxm, hxp, hym, hyp, hzm, hzp)
    sweep(buf, other, coefs, source, AFTER[0])
    sweep(other, buf, coefs, source, AFTER[1])
    sweep(buf, other, coefs, source, AFTER[2])
    sweep(other, buf, coefs, source, AFTER[3])
    for sub in range(8):
        block = buf[pl.ds(STEP + sub, BZ, stride=8), :].T
        for g in (1, 2):
            x = 8 * g - 8 + sub
            own = block[32 * g + 8 : 32 * g + 24]
            if split:
                outs[0][0, x] = own[:8]
                outs[1][0, x] = own[8:]
            else:
                outs[0][x] = own


def ring(value, axis, size, by):
    return lax.ppermute(value, axis, [(n, (n + by) % size) for n in range(size)])


def from_both(low, high, axis, size):
    return ring(high, axis, size, 1), ring(low, axis, size, -1)


def spread_planes(own_lo, own_hi):
    y_lo, y_hi = from_both(own_lo, own_hi, "gy", NGY)
    lows = [part[:, :8] for part in (y_lo, own_lo, own_hi, y_hi)]
    highs = [part[:, 8:] for part in (y_lo, own_lo, own_hi, y_hi)]
    x_lo, x_hi = from_both(
        jnp.concatenate(lows, axis=2), jnp.concatenate(highs, axis=2), "gx", NGX
    )
    own, z_lo, z_hi = turn(own_lo, own_hi, y_lo, y_hi, x_lo, x_hi)
    return (own, *from_both(z_lo, z_hi, "gz", NGZ))


def everywhere(send):
    return lax.all_to_all(send, AXES, 0, 0, tiled=True)


def correct(rhs, u, coefs, source, *kept):
    outs = [(BX, BY, BZ)] if kept else [(1, BX, 8, 128)] * 2 + [(16, 6, 8, 128), (16, 8, 128)]
    return call(
        functools.partial(correct_kernel, not kept),
        outs,
        [(ROWS, 128), (ROWS, 128), (16, 8, 128), (8 * 24, 128)],
        rhs, u, *coefs, source, *kept,
    )


def body(right_side, conductivity):
    both = jnp.stack([right_side, conductivity])
    own, z_lo, z_hi = spread_planes(both[:, :, :8], both[:, :, 8:])
    *held, u1, u2, u3, u4, layers, clayers = call(
        inner_kernel, [(ROWS, 128)] * 12 + [(128, 128)] * 2, [], own, cost=COST
    )
    *coefs, source, weight, u, send = call(
        ends_kernel,
        [(ROWS, 128)] * 9 + [(DEVICES, 128)],
        [(128, 128)],
        own, z_lo, z_hi, u1, u2, u3, layers, clayers, *held, u4,
        aliases={8 + n: n for n in range(9)},
    )
    own_lo, own_hi, *kept = correct(everywhere(send), u, coefs, source)
    own, z_lo, z_hi = spread_planes(own_lo, own_hi)
    u1, u2, u3, u4, layers = call(
        inner_again_kernel,
        [(ROWS, 128)] * 4 + [(128, 128)],
        [],
        own, *coefs, source, weight, cost=COST,
    )
    u, send = call(
        ends_again_kernel,
        [(ROWS, 128), (DEVICES, 128)],
        [(128, 128)],
        own, z_lo, z_hi, u1, u2, u3, layers, *coefs, source, weight, u4,
        aliases={15: 0},
    )
    return correct(everywhere(send), u, coefs, source, *kept)[0]


def solution(mesh):
    return jax.shard_map(
        body,
        mesh=mesh,
        in_specs=(P("gx", "gy", "gz"), P("gx", "gy", "gz")),
        out_specs=P("gx", "gy", "gz"),
        check_vma=False,
    )
```
